32 devices in a mesh: grp: 2 (over x), seq: 16 (over z, y, core).
Axes of the slice: x: 2, y: 2, z: 4, core: 2. Of those that a mesh axis runs over, the one named last changes fastest.
Arguments:
- inputs: bfloat16 [16384, 2560], P(('grp', 'seq')), parts along dimension 0, may hold values from -0.625 to 0.625
- write_vectors: bfloat16 [16384, 128], P(('grp', 'seq')), parts along dimension 0, may hold values from -1.5 to 1.5
- read_vectors: bfloat16 [16384, 128], P(('grp', 'seq')), parts along dimension 0, may hold values from -1.5 to 1.5
- log_decay: float32 [40, 16384], P(None, ('grp', 'seq')), parts along dimension 1, may hold values from -1.5 to 0
- grad_out: bfloat16 [16384, 2560], P(('grp', 'seq')), parts along dimension 0, may hold values from -2 to 2
Outputs:
- grad_inputs: bfloat16 [16384, 2560], P(('grp', 'seq')), parts along dimension 0
- grad_write: bfloat16 [16384, 128], P(('grp', 'seq')), parts along dimension 0
- grad_read: bfloat16 [16384, 128], P(('grp', 'seq')), parts along dimension 0
- grad_decay: float32 [40, 16384], P(None, ('grp', 'seq')), parts along dimension 1
The draws below stay inside these ranges and needn't reach their ends.
There are 2 independent parts, one for each index of `grp`. The reference program is written for one: setup_inputs(seed, part) draws one part's arguments, and reference() takes and returns one part's arrays. A program takes and returns all parts, laid end to end along the dimension named above; each array names one. Nothing has to cross between parts.
All inputs are finite; a program needn't handle non-finite values.
Results may differ from the reference program's by a relative error of at most 0.008.
Values sent between devices are 32-bit elements; how exact they have to be, the bound alone decides.
A program may use at most 128 MiB of HBM per device.

```python
import math
import jax
import jax.numpy as jnp
from jax import lax

HEADS = 40
P_SIZE = 64
N = 128
BLOCK = 512
TOK_DEV = 512
SEQUENCE_LENGTH = 8192


def draw_log_decay(key, part):
    random_keys = jax.random.split(key, 7)
    choose = jax.random.uniform(random_keys[0], (HEADS, 1))
    slow_heads = choose < 0.5
    slow_rate = jnp.exp(jax.random.uniform(random_keys[1], (HEADS, 1), minval=math.log(0.05), maxval=math.log(0.3))) / SEQUENCE_LENGTH
    fast_rate = jnp.exp(jax.random.uniform(random_keys[2], (HEADS, 1), minval=math.log(1.0 / 45.0), maxval=math.log(1.0 / 30.0)))
    baseline_decay_rate = jnp.where(slow_heads, slow_rate, fast_rate)
    multiplier = jnp.exp(jax.random.uniform(random_keys[3], (HEADS, SEQUENCE_LENGTH // TOK_DEV), minval=-math.log(2.0), maxval=math.log(2.0)))
    multiplier = jnp.repeat(multiplier, TOK_DEV, axis=1)
    jitter_level = jax.random.uniform(random_keys[4], (HEADS, SEQUENCE_LENGTH), minval=0.5, maxval=1.5)
    spike_positions = jax.random.randint(random_keys[5], (2,), 0, SEQUENCE_LENGTH)
    spike_amount = jax.random.uniform(random_keys[6], (HEADS, 2), minval=0.22, maxval=0.6)
    sequence_position = jnp.arange(SEQUENCE_LENGTH)
    spike_values = jnp.where(sequence_position[None, :] == spike_positions[0], spike_amount[:, 0:1], 0.0) + jnp.where(sequence_position[None, :] == spike_positions[1], spike_amount[:, 1:2], 0.0)
    return (-(baseline_decay_rate * multiplier * jitter_level) - spike_values).astype(jnp.float32)


def levels(stream_key, extent, shards, smallest, high):
    gain = 1.0
    for position, shards_of in shards:
        draws = jax.random.uniform(jax.random.fold_in(jax.random.fold_in(stream_key, 6), position), (shards_of,), jnp.float32, smallest / len(shards), high / len(shards))
        gain = gain * jnp.repeat(jnp.exp(draws), extent[position] // shards_of).reshape((-1,) + (1,) * (len(extent) - 1 - position))
    return gain


def gaussian(key, extent, spread, most, shards=(), held_as=jnp.bfloat16):
    values = spread * jax.random.normal(key, extent, jnp.float32)
    if shards:
        values = values * levels(key, extent, shards, -0.22, 0.18)
    return jnp.clip(values, -most, most).astype(held_as)


def setup_inputs(seed: int = 0, part: int = 0) -> dict:
    splits = jax.random.split(jax.random.key(seed), 6)
    own_keys = jax.random.split(jax.random.fold_in(splits[5], part), 6)
    return {
        "inputs": gaussian(own_keys[0], (SEQUENCE_LENGTH, HEADS * P_SIZE), (4.0 * SEQUENCE_LENGTH ** -0.5), 0.625, ((0, 16),)),
        "write_vectors": gaussian(own_keys[1], (SEQUENCE_LENGTH, N), 0.1, 1.5, ((0, 16),)),
        "read_vectors": gaussian(own_keys[2], (SEQUENCE_LENGTH, N), 0.1, 1.5, ((0, 16),)),
        "log_decay": draw_log_decay(jax.random.fold_in(jax.random.fold_in(splits[5], part), 71), part),
        "grad_out": gaussian(own_keys[4], (SEQUENCE_LENGTH, HEADS * P_SIZE), (12.0 * SEQUENCE_LENGTH ** -0.5), 2.0, ((0, 16),)),
    }


def reference(inputs, write_vectors, read_vectors, log_decay, grad_out):
    blocks = SEQUENCE_LENGTH // BLOCK
    input_heads = inputs.reshape(blocks, BLOCK, HEADS, P_SIZE)
    grad_heads = grad_out.reshape(blocks, BLOCK, HEADS, P_SIZE)
    write_blocks = write_vectors.reshape(blocks, BLOCK, N)
    read_blocks = read_vectors.reshape(blocks, BLOCK, N)
    rate_rows = log_decay.reshape(HEADS, blocks, BLOCK).transpose(1, 0, 2)
    cumulative = jnp.cumsum(rate_rows, axis=2)
    last_cum = cumulative[:, :, BLOCK - 1:]
    growth_pos = jnp.exp(cumulative).transpose(0, 2, 1)[..., None]
    tail_pos = jnp.exp(last_cum - cumulative).transpose(0, 2, 1)[..., None]
    weighted_in = (input_heads.astype(jnp.float32) * tail_pos).astype(jnp.bfloat16)
    weighted_grad = (grad_heads.astype(jnp.float32) * growth_pos).astype(jnp.bfloat16)
    local_state = jnp.einsum('kqn,kqhp->khnp', write_blocks.astype(jnp.float32), weighted_in.astype(jnp.float32))
    local_adjoint = jnp.einsum('kqn,kqhp->khnp', read_blocks.astype(jnp.float32), weighted_grad.astype(jnp.float32))
    block_decay = jnp.exp(last_cum[:, :, 0])

    def carry_step(carried, pieces):
        decay_here, local_here = pieces
        return decay_here[:, None, None] * carried + local_here, carried

    empty_state = jnp.zeros((HEADS, N, P_SIZE), jnp.float32)
    _, enter_block = lax.scan(carry_step, empty_state, (block_decay, local_state))
    _, leave_block = lax.scan(carry_step, empty_state, (block_decay, local_adjoint), reverse=True)
    positions = jnp.arange(BLOCK)
    lower_mask = positions[:, None] >= positions[None, :]

    def per_block(pieces):
        block_in, block_grad, block_write, block_read, block_cum, block_last, enter_here, leave_here, decay_here, local_here = pieces
        inputs_f = block_in.astype(jnp.float32)
        grads_f = block_grad.astype(jnp.float32)
        scores = jnp.dot(block_read, block_write.T, preferred_element_type=jnp.float32)
        cum_gap = block_cum[:, :, None] - block_cum[:, None, :]
        decay_mat = jnp.exp(jnp.where(lower_mask[None], cum_gap, -jnp.inf))
        mixing = lax.optimization_barrier((scores[None] * decay_mat).astype(jnp.bfloat16)).astype(jnp.float32)
        growth_here = jnp.exp(block_cum).T[..., None]
        tail_here = jnp.exp(block_last - block_cum).T[..., None]
        head_out = jnp.einsum('htu,uhp->thp', mixing, inputs_f) + jnp.einsum('tn,hnp->thp', block_read.astype(jnp.float32), enter_here, precision=lax.Precision.HIGHEST) * growth_here
        input_back = jnp.einsum('htu,thp->uhp', mixing, grads_f) + jnp.einsum('un,hnp->uhp', block_write.astype(jnp.float32), leave_here, precision=lax.Precision.HIGHEST) * tail_here
        flow_terms = (jnp.sum(grads_f * head_out, axis=2) - jnp.sum(inputs_f * input_back, axis=2)).T
        suffix = jnp.flip(jnp.cumsum(jnp.flip(flow_terms, 1), axis=1), 1)
        end_state = decay_here[:, None, None] * enter_here + local_here
        grad_decay = suffix + jnp.sum(end_state * leave_here, axis=(1, 2))[:, None]
        pair_sum = jnp.sum(jnp.einsum('thp,uhp->htu', grads_f, inputs_f) * decay_mat, axis=0).astype(jnp.bfloat16)
        grad_read = jnp.dot(pair_sum, block_write, preferred_element_type=jnp.float32) + jnp.einsum('thp,hnp->tn', grads_f * growth_here, enter_here, precision=lax.Precision.HIGHEST)
        grad_write = jnp.dot(pair_sum.T, block_read, preferred_element_type=jnp.float32) + jnp.einsum('uhp,hnp->un', inputs_f * tail_here, leave_here, precision=lax.Precision.HIGHEST)
        return (input_back.reshape(BLOCK, HEADS * P_SIZE).astype(jnp.bfloat16), grad_write.astype(jnp.bfloat16), grad_read.astype(jnp.bfloat16), grad_decay)

    grad_inputs, grad_write, grad_read, grad_decay = lax.map(per_block, (input_heads, grad_heads, write_blocks, read_blocks, cumulative, last_cum, enter_block, leave_block, block_decay, local_state))
    return (grad_inputs.reshape(SEQUENCE_LENGTH, HEADS * P_SIZE), grad_write.reshape(SEQUENCE_LENGTH, N), grad_read.reshape(SEQUENCE_LENGTH, N), grad_decay.transpose(1, 0, 2).reshape(HEADS, SEQUENCE_LENGTH))
```

```python
import functools
import jax
import jax.numpy as jnp
from jax import lax
from jax.experimental import pallas as pl
from jax.experimental.pallas import tpu as pltpu
from jax.sharding import PartitionSpec as P

HEADS = 40
P_SIZE = 64
N = 128
BLOCK = 512
WIDTH = HEADS * P_SIZE
QUARTERS = 4
QUARTER = WIDTH // QUARTERS
PAY = 2 * N + 8
CHUNK = 128
CHUNKS = QUARTER // CHUNK
F32 = jnp.float32
BF16 = jnp.bfloat16
VMEM_BYTES = 50 * 1024 * 1024
COPY_BYTES = 1024 * 1024


def split_two(values):
    upper = values.astype(BF16)
    return upper, (values - upper.astype(F32)).astype(BF16)


def split_three(values):
    upper = values.astype(BF16)
    rest = values - upper.astype(F32)
    middle = rest.astype(BF16)
    return upper, middle, (rest - middle.astype(F32)).astype(BF16)


def contract(left, right, left_dim, right_dim):
    return lax.dot_general(
        left, right, (((left_dim,), (right_dim,)), ((), ())), preferred_element_type=F32
    )


def lower_ones():
    rows = lax.broadcasted_iota(jnp.int32, (BLOCK, BLOCK), 0)
    columns = lax.broadcasted_iota(jnp.int32, (BLOCK, BLOCK), 1)
    return jnp.where(rows >= columns, 1.0, 0.0).astype(BF16)


TILE = 256


def pair_step(j, x_ref, g_ref, cumx_ref, cumrow_ref, within_ref, outdot_ref, indot_ref,
              scores_ref, pairs_ref):
    column = pl.multiple_of(j * 128, 128)
    x = x_ref[:, pl.ds(column, 128)]
    g = g_ref[:, pl.ds(column, 128)]
    cum = cumx_ref[:, pl.ds(column, 128)]
    lanes = lax.broadcasted_iota(jnp.int32, (BLOCK, 128), 1)
    zero = jnp.zeros((), BF16)
    x_heads = [jnp.where(lanes < 64, x, zero), jnp.where(lanes >= 64, x, zero)]
    g_heads = [jnp.where(lanes < 64, g, zero), jnp.where(lanes >= 64, g, zero)]
    diagonal = lax.broadcasted_iota(jnp.int32, (TILE, TILE), 0) <= lax.broadcasted_iota(
        jnp.int32, (TILE, TILE), 1
    )
    tiles = BLOCK // TILE
    cum_columns = [cum[:, :1], cum[:, 64:65]]
    cum_rows = [cumrow_ref[pl.ds(2 * j + head, 1), :] for head in range(2)]
    out_sums = [[jnp.zeros((1, TILE), F32) for _ in range(tiles)] for _ in range(2)]
    for row in range(tiles):
        u = slice(row * TILE, (row + 1) * TILE)
        total = jnp.zeros((TILE, 128), F32)
        in_sums = [jnp.zeros((TILE, 128), F32) for _ in range(2)]
        for col in range(row, tiles):
            t = slice(col * TILE, (col + 1) * TILE)
            scores = scores_ref[u, t]
            added = pairs_ref[u, t]
            for head in range(2):
                gap = cum_rows[head][:, t] - cum_columns[head][u]
                if row == col:
                    gap = jnp.where(diagonal, gap, -jnp.inf)
                decay = jnp.exp(gap)
                products = contract(x_heads[head][u], g[t], 1, 1)
                decayed = products * decay
                added = added + decayed
                mixing = (scores * decay).astype(BF16)
                total = total + contract(mixing, g_heads[head][t], 1, 0)
                flow = scores * decayed
                out_sums[head][col] = out_sums[head][col] + jnp.sum(flow, axis=0, keepdims=True)
                for lane in range(TILE // 128):
                    in_sums[head] = in_sums[head] + flow[:, lane * 128 : (lane + 1) * 128]
            pairs_ref[u, t] = added
        within_ref[u, pl.ds(column, 128)] = total
        lane_index = lax.broadcasted_iota(jnp.int32, (TILE, 128), 1)
        gathered = indot_ref[u, :]
        for head in range(2):
            gathered = jnp.where(
                lane_index == 2 * j + head, jnp.sum(in_sums[head], axis=1, keepdims=True), gathered
            )
        indot_ref[u, :] = gathered
    for head in range(2):
        for col in range(tiles):
            outdot_ref[pl.ds(2 * j + head, 1), col * TILE : (col + 1) * TILE] = out_sums[head][col]


def parts_of(pay):
    return pay[:N], pay[N : 2 * N], pay[2 * N : 2 * N + 1]


def join(early, late, out_ref, index):
    early_s, early_r, early_d = parts_of(early)
    late_s, late_r, late_d = parts_of(late)
    out_ref[index, :N] = late_d * early_s + late_s
    out_ref[index, N : 2 * N] = early_r + early_d * late_r
    out_ref[index, 2 * N :] = jnp.broadcast_to(early_d * late_d, (8, CHUNK))


def ordered(is_late, mine, other):
    return jnp.where(is_late, other, mine), jnp.where(is_late, mine, other)


def descend(is_late, mine, other, enter, leave):
    early, late = ordered(is_late, mine, other)
    early_s, _, early_d = parts_of(early)
    _, late_r, late_d = parts_of(late)
    first_leave = late_r + late_d * leave
    second_enter = early_d * enter + early_s
    own = (jnp.where(is_late, second_enter, enter), jnp.where(is_late, leave, first_leave))
    far = (jnp.where(is_late, enter, second_enter), jnp.where(is_late, first_leave, leave))
    return own, far


JOIN_START = 4
FIRST_START = 8
SECOND_START = 13
DOWN_START = 17
NEAR_START = 19
FAR_START = 22
SLOTS = FAR_START + 2 * CHUNKS - 1


def whole_kernel(ranks, x_ref, g_ref, b_ref, c_ref, rate_ref,
                 grad_ref, write_ref, read_ref, decay_ref,
                 cumx_ref, within_ref, cumrow_ref, outdot_ref, indot_ref, flow_ref, ends_ref,
                 read_sum, write_sum, cum_parts, b_turned, c_turned, pay_ref, carry_ref,
                 scores_ref, pairs_ref, core_in, pair_buf, row_in, group_buf, enter_in, enter_out,
                 leave_in, leave_out, down_out, down_in, back_out, back_in,
                 core_send, core_recv, row_send, row_recv, enter_send, enter_recv, leave_send,
                 leave_recv, down_send, down_recv, back_send, back_recv):
    me = lax.axis_index("seq")
    core = lax.rem(me, 2)
    row = lax.rem(me // 2, 2)
    rank = me // 4
    core_peer = me + 1 - 2 * core
    row_peer = me + 2 - 4 * row
    is_first, is_last = rank == 0, rank == ranks - 1
    is_lower = rank < ranks // 2

    def remote(source, target, send, recv, peer):
        return pltpu.make_async_remote_copy(
            src_ref=source, dst_ref=target, send_sem=send, recv_sem=recv,
            device_id={"seq": peer}, device_id_type=pl.DeviceIdType.MESH,
        )

    def core_copy(r, k):
        mine = (2 * (1 - core) + r) * CHUNKS + k
        slot = r * CHUNKS + k
        return remote(pay_ref.at[mine], core_in.at[slot], core_send.at[slot], core_recv.at[slot],
                      core_peer)

    def row_copy(k):
        return remote(pair_buf.at[(1 - row) * CHUNKS + k], row_in.at[k], row_send.at[k],
                      row_recv.at[k], row_peer)

    def enter_copy(k):
        return remote(enter_out.at[k], enter_in.at[k], enter_send.at[k], enter_recv.at[k], me + 4)

    def leave_copy(k):
        return remote(leave_out.at[k], leave_in.at[k], leave_send.at[k], leave_recv.at[k], me - 4)

    def down_copy(k):
        return remote(down_out.at[k], down_in.at[k], down_send.at[k], down_recv.at[k], row_peer)

    def back_copy(r, k):
        slot = r * CHUNKS + k
        return remote(back_out.at[slot], back_in.at[slot], back_send.at[slot], back_recv.at[slot],
                      core_peer)

    barrier = pltpu.get_barrier_semaphore()

    def greet(peer):
        pl.semaphore_signal(barrier, inc=1, device_id={"seq": peer},
                            device_id_type=pl.DeviceIdType.MESH)

    greet(core_peer)
    greet(row_peer)

    @pl.when(jnp.logical_not(is_first))
    def _():
        greet(me - 4)

    @pl.when(jnp.logical_not(is_last))
    def _():
        greet(me + 4)

    chain_peers = jnp.where(is_first, 0, 1) + jnp.where(is_last, 0, 1)
    pl.semaphore_wait(barrier, 2 + chain_peers)

    lower = lower_ones()
    rates = rate_ref[...]
    rate_parts = split_three(rates)
    cumrow_ref[...] = sum(contract(part, lower, 1, 1) for part in rate_parts)
    padded = jnp.concatenate([rates, rates, rates, jnp.zeros((8, BLOCK), F32)], axis=0)
    columns = sum(contract(lower, part, 1, 1) for part in split_three(padded))
    lanes = lax.broadcasted_iota(jnp.int32, (BLOCK, 128), 1)
    upper, middle, rest = [part.astype(F32) for part in split_three(columns)]
    cum_parts[...] = jnp.where(
        lanes < HEADS, upper, jnp.where(lanes < 2 * HEADS, middle, rest)
    ).astype(BF16)
    b_turned[...] = b_ref[...].astype(F32).T.astype(BF16)
    c_turned[...] = c_ref[...].astype(F32).T.astype(BF16)

    def local_chunk(chunk):
        column = pl.multiple_of(chunk * CHUNK, CHUNK)
        source = lax.broadcasted_iota(jnp.int32, (128, 128), 0)
        target = lax.broadcasted_iota(jnp.int32, (128, 128), 1)
        head = 2 * chunk + jnp.where(target >= P_SIZE, 1, 0)
        match = (source == head) | (source == head + HEADS) | (source == head + 2 * HEADS)
        spread = jnp.where(match, 1.0, 0.0).astype(BF16)
        cumx = contract(cum_parts[...], spread, 1, 0)
        cumx_ref[:, pl.ds(column, CHUNK)] = cumx
        last = cumx[BLOCK - 1 :, :]
        x = x_ref[:, pl.ds(column, CHUNK)].astype(F32)
        g = g_ref[:, pl.ds(column, CHUNK)].astype(F32)
        x_weighted = (x * jnp.exp(last - cumx)).astype(BF16)
        g_weighted = (g * jnp.exp(cumx)).astype(BF16)
        pay_ref[chunk, :N] = contract(b_turned[...], x_weighted, 1, 0)
        pay_ref[chunk, N : 2 * N] = contract(c_turned[...], g_weighted, 1, 0)
        pay_ref[chunk, 2 * N :] = jnp.broadcast_to(jnp.exp(last), (8, CHUNK))

    @pl.loop(0, CHUNKS)
    def _(k):
        @pl.loop(0, 2)
        def _(step):
            r = jnp.where(step == 0, 1 - row, row)
            local_chunk((2 * (1 - core) + r) * CHUNKS + k)
            core_copy(r, k).start()

    scores_ref[...] = contract(b_ref[...], c_ref[...], 1, 1)
    pairs_ref[...] = jnp.zeros_like(pairs_ref)
    indot_ref[...] = jnp.zeros_like(indot_ref)
    flow_ref[...] = jnp.zeros_like(flow_ref)
    ends_ref[...] = jnp.zeros_like(ends_ref)
    read_sum[...] = jnp.zeros_like(read_sum)
    write_sum[...] = jnp.zeros_like(write_sum)
    is_core_late, is_row_late = core == 1, row == 1

    def pair_join(r, k):
        core_copy(r, k).wait_recv()
        slot = r * CHUNKS + k
        early, late = ordered(is_core_late, pay_ref[(2 * core + r) * CHUNKS + k], core_in[slot])
        join(early, late, pair_buf, slot)

    def send_enter(k, enter):
        enter_out[k] = group_buf[k, 2 * N : 2 * N + 1] * enter + group_buf[k, :N]
        enter_copy(k).start()

    def send_leave(k, leave):
        leave_out[k] = group_buf[k, 2 * N : 2 * N + 1] * leave + group_buf[k, N : 2 * N]
        leave_copy(k).start()

    def take_enter(k):
        @pl.when(is_first)
        def _():
            enter_in[k] = jnp.zeros((N, CHUNK), F32)

        @pl.when(jnp.logical_not(is_first))
        def _():
            enter_copy(k).wait_recv()

        @pl.when(jnp.logical_not(is_last))
        def _():
            send_enter(k, enter_in[k])

    def take_leave(k):
        @pl.when(is_last)
        def _():
            leave_in[k] = jnp.zeros((N, CHUNK), F32)

        @pl.when(jnp.logical_not(is_last))
        def _():
            leave_copy(k).wait_recv()

        @pl.when(jnp.logical_not(is_first))
        def _():
            send_leave(k, leave_in[k])

    def final_level(r, k, enter, leave):
        slot = r * CHUNKS + k
        mine = (2 * core + r) * CHUNKS + k
        own, far = descend(is_core_late, pay_ref[mine], core_in[slot], enter, leave)
        carry_ref[mine, :N], carry_ref[mine, N:] = own
        back_out[slot, :N], back_out[slot, N:] = far
        back_copy(r, k).start()

    def up(k):
        pair_join(1 - row, k)
        row_copy(k).start()
        pair_join(row, k)

    def group_join(k):
        row_copy(k).wait_recv()
        early, late = ordered(is_row_late, pair_buf[row * CHUNKS + k], row_in[k])
        join(early, late, group_buf, k)

        @pl.when(is_first)
        def _():
            take_enter(k)

        @pl.when(is_last)
        def _():
            take_leave(k)

    def first_pass(k):
        @pl.when(jnp.logical_and(is_lower, jnp.logical_not(is_first)))
        def _():
            take_enter(k)

        @pl.when(jnp.logical_not(jnp.logical_or(is_lower, is_last)))
        def _():
            take_leave(k)

    def final_chunk(chunk):
        column = pl.multiple_of(chunk * CHUNK, CHUNK)
        cumx = cumx_ref[:, pl.ds(column, CHUNK)]
        tail = jnp.exp(cumx[BLOCK - 1 :, :] - cumx)
        x_tail = x_ref[:, pl.ds(column, CHUNK)].astype(F32) * tail
        g_growth = g_ref[:, pl.ds(column, CHUNK)].astype(F32) * jnp.exp(cumx)
        enter = carry_ref[chunk, :N]
        leave = carry_ref[chunk, N:]
        enter_two = jnp.concatenate(split_two(enter), axis=0)
        leave_two = jnp.concatenate(split_two(leave), axis=0)
        enter_wide = jnp.concatenate(split_two(enter), axis=1)
        leave_wide = jnp.concatenate(split_two(leave), axis=1)
        b, c = b_ref[...], c_ref[...]
        out = contract(jnp.concatenate([c, c], axis=1), enter_two, 1, 0)
        back = contract(jnp.concatenate([b, b], axis=1), leave_two, 1, 0)
        grad_ref[:, pl.ds(column, CHUNK)] = (
            within_ref[:, pl.ds(column, CHUNK)] + back * tail
        ).astype(BF16)
        g_high, x_high = g_growth.astype(BF16), x_tail.astype(BF16)
        read_sum[...] += contract(jnp.concatenate([g_high, g_high], axis=1), enter_wide, 1, 1)
        write_sum[...] += contract(jnp.concatenate([x_high, x_high], axis=1), leave_wide, 1, 1)
        flow = jnp.concatenate(split_two(g_growth * out - x_tail * back), axis=1)
        source = lax.broadcasted_iota(jnp.int32, (256, 128), 0)
        target = lax.broadcasted_iota(jnp.int32, (256, 128), 1)
        head = 2 * chunk + lax.rem(source // P_SIZE, 2)
        gather = jnp.where(target == head, 1.0, 0.0).astype(BF16)
        flow_ref[...] += contract(flow, gather, 1, 0)
        end_state = pay_ref[chunk, 2 * N : 2 * N + 1] * enter + pay_ref[chunk, :N]
        ends_ref[pl.ds(chunk, 1), :] = jnp.sum(end_state * leave, axis=0, keepdims=True)

    def second_pass(k):
        @pl.when(is_lower)
        def _():
            take_leave(k)

        @pl.when(jnp.logical_not(is_lower))
        def _():
            take_enter(k)

        own, far = descend(is_row_late, pair_buf[row * CHUNKS + k], row_in[k], enter_in[k],
                           leave_in[k])
        down_out[k, :N], down_out[k, N:] = far
        down_copy(k).start()
        final_level(row, k, *own)
        final_chunk((2 * core + row) * CHUNKS + k)

    def down(k):
        down_copy(k).wait_recv()
        final_level(1 - row, k, down_in[k, :N], down_in[k, N:])
        final_chunk((2 * core + 1 - row) * CHUNKS + k)

    def take_back(r, k):
        chunk = (2 * (1 - core) + r) * CHUNKS + k
        back_copy(r, k).wait_recv()
        carry_ref[chunk] = back_in[r * CHUNKS + k]
        final_chunk(chunk)

    @pl.loop(0, CHUNKS)
    def _(k):
        local_chunk((2 * core + 1 - row) * CHUNKS + k)
        local_chunk((2 * core + row) * CHUNKS + k)
        up(k)

    def stage(j, start, spacing, act):
        k = (j - start) // spacing
        due = (j >= start) & (j < start + spacing * CHUNKS) & (lax.rem(j - start, spacing) == 0)

        @pl.when(due)
        def _():
            act(k)

    @pl.loop(0, SLOTS)
    def _(j):
        stage(j, JOIN_START, 2, group_join)
        stage(j, FIRST_START, 2, first_pass)

        @pl.when(j < HEADS // 2)
        def _():
            half = jnp.where(j < 2 * CHUNKS, core, 1 - core)
            step = lax.rem(j, 2 * CHUNKS)
            r = jnp.where(step < CHUNKS, row, 1 - row)
            chunk = (2 * half + r) * CHUNKS + lax.rem(step, CHUNKS)
            pair_step(chunk, x_ref, g_ref, cumx_ref, cumrow_ref, within_ref, outdot_ref, indot_ref,
                      scores_ref, pairs_ref)

        stage(j, SECOND_START, 2, second_pass)
        stage(j, DOWN_START, 2, down)
        stage(j, NEAR_START, 2, functools.partial(take_back, row))
        stage(j, FAR_START, 2, functools.partial(take_back, 1 - row))

    pairs = pairs_ref[...].astype(BF16)
    read_ref[...] = (read_sum[...] + contract(pairs, b_ref[...], 0, 0)).astype(BF16)
    write_ref[...] = (write_sum[...] + contract(pairs, c_ref[...], 1, 0)).astype(BF16)
    heads = lax.broadcasted_iota(jnp.int32, (HEADS, 32), 0)
    chunks = lax.broadcasted_iota(jnp.int32, (HEADS, 32), 1)
    pick = jnp.where(heads // 2 == chunks, 1.0, 0.0).astype(BF16)
    ends = sum(contract(pick, part, 1, 0) for part in split_three(ends_ref[...]))
    heads = lax.broadcasted_iota(jnp.int32, (HEADS, 128), 0)
    entries = lax.broadcasted_iota(jnp.int32, (HEADS, 128), 1)
    own_head = entries // P_SIZE == lax.rem(heads, 2)
    total = jnp.sum(jnp.where(own_head, ends, 0.0), axis=1, keepdims=True)
    flows = (flow_ref[...] - indot_ref[...])[:, :HEADS]
    lower = lower_ones()
    total = total + sum(contract(part, lower, 0, 0) for part in split_three(flows))
    total = total + sum(contract(part, lower, 1, 0) for part in split_three(outdot_ref[...]))
    decay_ref[...] = total

    @pl.loop(0, CHUNKS)
    def _(k):
        for r in range(2):
            back_copy(r, k).wait_send()
            core_copy(r, k).wait_send()
        row_copy(k).wait_send()
        down_copy(k).wait_send()

        @pl.when(jnp.logical_not(is_last))
        def _():
            enter_copy(k).wait_send()

        @pl.when(jnp.logical_not(is_first))
        def _():
            leave_copy(k).wait_send()


def whole_call(x, g, b, c, rates, ranks):
    half, one = 2 * CHUNKS, CHUNKS

    def buffer(count, rows):
        return pltpu.VMEM((count, rows, CHUNK), F32)

    counts = [half, half] + [one] * 8 + [half, half]
    return pl.pallas_call(
        functools.partial(whole_kernel, ranks),
        out_shape=[
            jax.ShapeDtypeStruct((BLOCK, WIDTH), BF16),
            jax.ShapeDtypeStruct((BLOCK, N), BF16),
            jax.ShapeDtypeStruct((BLOCK, N), BF16),
            jax.ShapeDtypeStruct((HEADS, BLOCK), F32),
        ],
        in_specs=[pl.BlockSpec(memory_space=pltpu.VMEM)] * 5,
        out_specs=[pl.BlockSpec(memory_space=pltpu.VMEM)] * 4,
        scratch_shapes=[
            pltpu.VMEM((BLOCK, WIDTH), F32),
            pltpu.VMEM((BLOCK, WIDTH), F32),
            pltpu.VMEM((HEADS, BLOCK), F32),
            pltpu.VMEM((HEADS, BLOCK), F32),
            pltpu.VMEM((BLOCK, 128), F32),
            pltpu.VMEM((BLOCK, 128), F32),
            pltpu.VMEM((32, CHUNK), F32),
            pltpu.VMEM((BLOCK, N), F32),
            pltpu.VMEM((BLOCK, N), F32),
            pltpu.VMEM((BLOCK, 128), BF16),
            pltpu.VMEM((N, BLOCK), BF16),
            pltpu.VMEM((N, BLOCK), BF16),
            buffer(2 * half, PAY),
            buffer(2 * half, 2 * N),
            pltpu.VMEM((BLOCK, BLOCK), F32),
            pltpu.VMEM((BLOCK, BLOCK), F32),
            buffer(half, PAY), buffer(half, PAY), buffer(one, PAY), buffer(one, PAY),
            buffer(one, N), buffer(one, N), buffer(one, N), buffer(one, N),
            buffer(one, 2 * N), buffer(one, 2 * N), buffer(half, 2 * N), buffer(half, 2 * N),
        ] + [pltpu.SemaphoreType.DMA((count,)) for count in counts],
        compiler_params=pltpu.CompilerParams(
            vmem_limit_bytes=VMEM_BYTES, collective_id=0, has_side_effects=True
        ),
    )(x, g, b, c, rates)


def store_kernel(*refs):
    sources, targets, sems = refs[:4], refs[4:8], refs[8]
    copies = [
        pltpu.make_async_copy(source, target, sems.at[index])
        for index, (source, target) in enumerate(zip(sources, targets))
    ]
    for copy in copies:
        copy.start()
    for copy in copies:
        copy.wait()


def store_call(results):
    return pl.pallas_call(
        store_kernel,
        out_shape=[jax.ShapeDtypeStruct(result.shape, result.dtype) for result in results],
        in_specs=[pl.BlockSpec(memory_space=pl.ANY)] * 4,
        out_specs=[pl.BlockSpec(memory_space=pl.ANY)] * 4,
        scratch_shapes=[pltpu.SemaphoreType.DMA((4,))],
        compiler_params=pltpu.CompilerParams(vmem_limit_bytes=COPY_BYTES),
    )(*results)


def body(inputs, write_vectors, read_vectors, log_decay, grad_out, *, seq_size):
    results = whole_call(
        inputs, grad_out, write_vectors, read_vectors, log_decay, seq_size // 4
    )
    return tuple(store_call(results))


def solution(mesh):
    rows = P(("grp", "seq"), None)
    columns = P(None, ("grp", "seq"))
    return jax.shard_map(
        functools.partial(body, seq_size=mesh.shape["seq"]),
        mesh=mesh,
        in_specs=(rows, rows, rows, columns, rows),
        out_specs=(rows, rows, rows, columns),
        check_vma=False,
    )
```

```python
import functools
import jax
import jax.numpy as jnp
from jax import lax
from jax.experimental import pallas as pl
from jax.experimental.pallas import tpu as pltpu
from jax.sharding import PartitionSpec as P

HEADS = 40
P_SIZE = 64
N = 128
BLOCK = 512
WIDTH = HEADS * P_SIZE
CHUNK = 128
WIDE = 256
CHUNKS = WIDTH // (4 * CHUNK)
WIDES = WIDTH // WIDE
SUB = 128
PAY = 2 * N + 8
LOG2E = 1.4426950408889634
F32 = jnp.float32
BF16 = jnp.bfloat16
VMEM_BYTES = 53 * 1024 * 1024
COPY_BYTES = 1024 * 1024


def split_two(values):
    upper = values.astype(BF16)
    return upper, (values - upper.astype(F32)).astype(BF16)


def split_three(values):
    upper = values.astype(BF16)
    rest = values - upper.astype(F32)
    middle = rest.astype(BF16)
    return upper, middle, (rest - middle.astype(F32)).astype(BF16)


def contract(left, right, left_dim, right_dim):
    return lax.dot_general(
        left, right, (((left_dim,), (right_dim,)), ((), ())), preferred_element_type=F32
    )


def lower_ones():
    rows = lax.broadcasted_iota(jnp.int32, (BLOCK, BLOCK), 0)
    columns = lax.broadcasted_iota(jnp.int32, (BLOCK, BLOCK), 1)
    return jnp.where(rows >= columns, 1.0, 0.0).astype(BF16)


def parts_of(pay):
    return pay[:N], pay[N : 2 * N], pay[2 * N : 2 * N + 1]


def join(early, late, out_ref, index):
    early_s, early_r, early_d = parts_of(early)
    late_s, late_r, late_d = parts_of(late)
    out_ref[index, :N] = late_d * early_s + late_s
    out_ref[index, N : 2 * N] = early_r + early_d * late_r
    out_ref[index, 2 * N :] = jnp.broadcast_to(early_d * late_d, (8, CHUNK))


def ordered(is_late, mine, other):
    return jnp.where(is_late, other, mine), jnp.where(is_late, mine, other)


def descend(is_late, mine, other, enter, leave):
    early, late = ordered(is_late, mine, other)
    early_s, _, early_d = parts_of(early)
    _, late_r, late_d = parts_of(late)
    first_leave = late_r + late_d * leave
    second_enter = early_d * enter + early_s
    own = (jnp.where(is_late, second_enter, enter), jnp.where(is_late, leave, first_leave))
    far = (jnp.where(is_late, enter, second_enter), jnp.where(is_late, first_leave, leave))
    return own, far


JOIN_START = 0
SPACING = 3
HOP = 3
DOWN_LAG = 4
NEAR_LAG = 1
FAR_LAG = 5


def three_lanes(values):
    lanes = lax.broadcasted_iota(jnp.int32, values.shape, 1)
    upper, middle, rest = [part.astype(F32) for part in split_three(values)]
    picked = jnp.where(lanes < HEADS, upper, jnp.where(lanes < 2 * HEADS, middle, rest))
    return jnp.where(lanes < 3 * HEADS, picked, 0.0).astype(BF16)


def lane_pick(values, lane):
    index = jnp.full(values.shape, lane, jnp.int32)
    return jnp.take_along_axis(values, index, axis=1, mode="promise_in_bounds")


def whole_kernel(ranks, x_hbm, g_hbm, b_hbm, c_hbm, rate_hbm,
                 grad_ref, write_ref, read_ref, decay_ref,
                 x_ref, g_ref, b_ref, c_ref, rate_ref,
                 xw_ref, gw_ref, tail_ref, within_ref, flow_ref,
                 cumrow_ref, outdot_ref, flowrow_ref, ends_ref,
                 read_sum, write_sum, growth_parts, tail_parts, one_parts, two_parts, cum_ref,
                 heads_ref, b_turned, c_turned, pay_ref, carry_ref,
                 cross_ref, turned_ref, diag_ref, pairs_ref, core_in, pair_buf, row_in, group_buf,
                 enter_in, enter_out, leave_in, leave_out, down_out, down_in, back_out, back_in,
                 x_sem, g_sem, small_sem,
                 core_send, core_recv, row_send, row_recv, enter_send, enter_recv, leave_send,
                 leave_recv, down_send, down_recv, back_send, back_recv):
    me = lax.axis_index("seq")
    core = lax.rem(me, 2)
    row = lax.rem(me // 2, 2)
    rank = me // 4
    core_peer = me + 1 - 2 * core
    row_peer = me + 2 - 4 * row
    is_first, is_last = rank == 0, rank == ranks - 1

    def remote(source, target, send, recv, peer):
        return pltpu.make_async_remote_copy(
            src_ref=source, dst_ref=target, send_sem=send, recv_sem=recv,
            device_id={"seq": peer}, device_id_type=pl.DeviceIdType.MESH,
        )

    def chunk_of(r, k, q):
        return 4 * k + 2 * r + q

    def core_copy(r, k):
        slot = r * CHUNKS + k
        return remote(pay_ref.at[chunk_of(r, k, 1 - core)], core_in.at[slot], core_send.at[slot],
                      core_recv.at[slot], core_peer)

    def row_copy(k):
        return remote(pair_buf.at[(1 - row) * CHUNKS + k], row_in.at[k], row_send.at[k],
                      row_recv.at[k], row_peer)

    def enter_copy(k):
        return remote(enter_out.at[k], enter_in.at[k], enter_send.at[k], enter_recv.at[k], me + 4)

    def leave_copy(k):
        return remote(leave_out.at[k], leave_in.at[k], leave_send.at[k], leave_recv.at[k], me - 4)

    def down_copy(k):
        return remote(down_out.at[k], down_in.at[k], down_send.at[k], down_recv.at[k], row_peer)

    def back_copy(r, k):
        slot = r * CHUNKS + k
        return remote(back_out.at[slot], back_in.at[slot], back_send.at[slot], back_recv.at[slot],
                      core_peer)

    def wide_of(step):
        return 2 * lax.rem(step, CHUNKS) + jnp.where(step < CHUNKS, 1 - row, row)

    def columns_of(w):
        return pl.ds(pl.multiple_of(w * WIDE, WIDE), WIDE)

    def load(w):
        return (pltpu.make_async_copy(x_hbm.at[:, columns_of(w)], x_ref.at[:, columns_of(w)],
                                      x_sem.at[w]),
                pltpu.make_async_copy(g_hbm.at[:, columns_of(w)], g_ref.at[:, columns_of(w)],
                                      g_sem.at[w]))

    small = [pltpu.make_async_copy(source, target, small_sem.at[index])
             for index, (source, target) in enumerate(
                 ((rate_hbm, rate_ref), (b_hbm, b_ref), (c_hbm, c_ref)))]
    for copy in small:
        copy.start()

    @pl.loop(0, WIDES)
    def _(step):
        for copy in load(wide_of(step)):
            copy.start()

    barrier = pltpu.get_barrier_semaphore()

    def greet(peer):
        pl.semaphore_signal(barrier, inc=1, device_id={"seq": peer},
                            device_id_type=pl.DeviceIdType.MESH)

    greet(core_peer)
    greet(row_peer)

    @pl.when(jnp.logical_not(is_first))
    def _():
        greet(me - 4)

    @pl.when(jnp.logical_not(is_last))
    def _():
        greet(me + 4)

    source = lax.broadcasted_iota(jnp.int32, (128, WIDE), 0)
    target = lax.broadcasted_iota(jnp.int32, (128, WIDE), 1)
    head = source - jnp.where(source >= HEADS, HEADS, 0) - jnp.where(source >= 2 * HEADS, HEADS, 0)
    head = jnp.where(source < 3 * HEADS, head, 4 * HEADS)
    heads_ref[...] = head - target // P_SIZE

    small[0].wait()
    lower = lower_ones()
    rates = rate_ref[...] * LOG2E
    padded = jnp.concatenate([rates, rates, rates, jnp.zeros((8, BLOCK), F32)], axis=0)
    cum = sum(contract(lower, part, 1, 1) for part in split_three(padded))
    growth_parts[...] = three_lanes(jnp.exp2(cum))
    tail_parts[...] = three_lanes(jnp.exp2(cum[BLOCK - 1 :] - cum))
    for copy in small[1:]:
        copy.wait()
    b_turned[...] = b_ref[...].astype(F32).T.astype(BF16)
    c_turned[...] = c_ref[...].astype(F32).T.astype(BF16)
    cum_ref[...] = cum

    def local_wide(w):
        columns = columns_of(w)
        spread = jnp.where(heads_ref[...] == 4 * w, 1.0, 0.0).astype(BF16)
        growth = contract(growth_parts[...], spread, 1, 0)
        tail = contract(tail_parts[...], spread, 1, 0)
        x_weighted = (x_ref[:, columns].astype(F32) * tail).astype(BF16)
        g_weighted = (g_ref[:, columns].astype(F32) * growth).astype(BF16)
        xw_ref[:, columns] = x_weighted
        gw_ref[:, columns] = g_weighted
        tail_ref[:, columns] = tail
        state = contract(b_turned[...], x_weighted, 1, 0)
        adjoint = contract(c_turned[...], g_weighted, 1, 0)
        decay = jnp.broadcast_to(growth[BLOCK - 1 :], (8, WIDE))
        for q in range(2):
            lanes = slice(q * CHUNK, (q + 1) * CHUNK)
            pay_ref[2 * w + q, :N] = state[:, lanes]
            pay_ref[2 * w + q, N : 2 * N] = adjoint[:, lanes]
            pay_ref[2 * w + q, 2 * N :] = decay[:, lanes]

    is_core_late, is_row_late = core == 1, row == 1

    def pair_join(r, k):
        core_copy(r, k).wait_recv()
        slot = r * CHUNKS + k
        early, late = ordered(is_core_late, pay_ref[chunk_of(r, k, core)], core_in[slot])
        join(early, late, pair_buf, slot)

    chain_peers = jnp.where(is_first, 0, 1) + jnp.where(is_last, 0, 1)
    pl.semaphore_wait(barrier, 2 + chain_peers)

    @pl.loop(0, WIDES)
    def _(step):
        w = wide_of(step)
        for copy in load(w):
            copy.wait()
        local_wide(w)
        core_copy(lax.rem(w, 2), w // 2).start()

        @pl.when((step >= 1) & (step <= CHUNKS))
        def _():
            pair_join(1 - row, step - 1)
            row_copy(step - 1).start()

    one_parts[...] = three_lanes(jnp.exp2(-jnp.abs(cum - cum[2 * SUB - 1 : 2 * SUB])))
    two_parts[...] = three_lanes(jnp.exp2(-jnp.abs(cum - jnp.concatenate(
        [jnp.broadcast_to(cum[at : at + 1], (2 * SUB, 128)) for at in (SUB - 1, 3 * SUB - 1)],
        axis=0))))
    cumrow_ref[...] = sum(contract(part, lower, 1, 1) for part in split_three(rates))
    scores = contract(b_ref[...], c_ref[...], 1, 1)
    cross_ref[...] = scores.astype(BF16)
    turned_ref[...] = contract(c_ref[...], b_ref[...], 1, 1).astype(BF16)
    upper = lax.broadcasted_iota(jnp.int32, (SUB, SUB), 0) <= lax.broadcasted_iota(
        jnp.int32, (SUB, SUB), 1)
    for sub in range(4):
        rows = slice(sub * SUB, (sub + 1) * SUB)
        diag_ref[sub] = jnp.where(upper, scores[rows, rows], 0.0)
    pairs_ref[...] = jnp.zeros_like(pairs_ref)
    ends_ref[...] = jnp.zeros_like(ends_ref)
    read_sum[...] = jnp.zeros_like(read_sum)
    write_sum[...] = jnp.zeros_like(write_sum)

    def block_wide(w):
        columns = columns_of(w)
        spread = jnp.where(heads_ref[...] == 4 * w, 1.0, 0.0).astype(BF16)
        one = contract(one_parts[...], spread, 1, 0)
        two = contract(two_parts[...], spread, 1, 0)
        x, g = x_ref[:, columns], g_ref[:, columns]
        half = 2 * SUB
        x_one = (x[:half].astype(F32) * one[:half]).astype(BF16)
        g_one = (g[half:].astype(F32) * one[half:]).astype(BF16)
        pairs_ref[:half, half:] += contract(x_one, g_one, 1, 1)
        back_one = contract(cross_ref[:half, half:], g_one, 1, 0)
        out_one = contract(turned_ref[half:, :half], x_one, 1, 0)
        flow_one = [x_one.astype(F32) * back_one, g_one.astype(F32) * out_one]
        lanes = lax.broadcasted_iota(jnp.int32, (SUB, 128), 1)
        zero = jnp.zeros((), BF16)
        out_dots = [[] for _ in range(4)]
        cum_heads = [cumrow_ref[pl.ds(4 * w + h, 1), :] for h in range(4)]
        for side in range(2):
            early = slice(side * half, side * half + SUB)
            late = slice(side * half + SUB, (side + 1) * half)
            x_two = (x[early].astype(F32) * two[early]).astype(BF16)
            g_two = (g[late].astype(F32) * two[late]).astype(BF16)
            pairs_ref[early, late] += contract(x_two, g_two, 1, 1)
            back_two = contract(cross_ref[early, late], g_two, 1, 0)
            out_two = contract(turned_ref[late, early], x_two, 1, 0)
            flow_two = [-(x_two.astype(F32) * back_two), g_two.astype(F32) * out_two]
            for part, rows in enumerate((early, late)):
                local = slice(part * SUB, (part + 1) * SUB)
                if side == 0:
                    flow = flow_two[part] - flow_one[0][local]
                    within = one[rows] * back_one[local]
                    if part == 0:
                        within = within + two[rows] * back_two
                else:
                    flow = flow_two[part] + flow_one[1][local]
                    within = two[rows] * back_two if part == 0 else None
                sub = 2 * side + part
                scores = diag_ref[sub]
                scores = jnp.concatenate([scores, scores], axis=1)
                added = pairs_ref[rows, rows]
                for pair in range(2):
                    place = slice(pair * 128, (pair + 1) * 128)
                    xs, gs = x[rows, place], g[rows, place]
                    g_split = jnp.concatenate(
                        [jnp.where(lanes < P_SIZE, gs, zero), jnp.where(lanes >= P_SIZE, gs, zero)],
                        axis=0)
                    products = contract(xs, g_split, 1, 1)
                    gap = jnp.concatenate(
                        [lane_pick(cum_ref[rows, :], 4 * w + 2 * pair + h) for h in range(2)],
                        axis=1)
                    cum_rows = jnp.concatenate(
                        [cum_heads[2 * pair + h][:, rows] for h in range(2)],
                        axis=1)
                    decay = jnp.exp2(jnp.minimum(cum_rows - gap, 0.0))
                    decayed = products * decay
                    added = added + decayed[:, :SUB] + decayed[:, SUB:]
                    mixing = (scores * decay).astype(BF16)
                    out_dot = jnp.sum(mixing.astype(F32) * products, axis=0, keepdims=True)
                    for h in range(2):
                        out_dots[2 * pair + h].append(out_dot[:, h * SUB : (h + 1) * SUB])
                    back = contract(mixing, g_split, 1, 0)
                    at = pl.ds(pl.multiple_of(w * WIDE + pair * 128, 128), 128)
                    within_ref[rows, at] = back if within is None else within[:, place] + back
                    flow_ref[rows, at] = flow[:, place] - xs.astype(F32) * back
                pairs_ref[rows, rows] = added
        for h in range(4):
            outdot_ref[pl.ds(4 * w + h, 1), :] = jnp.concatenate(out_dots[h], axis=1)

    def send_enter(k, enter):
        enter_out[k] = group_buf[k, 2 * N : 2 * N + 1] * enter + group_buf[k, :N]
        enter_copy(k).start()

    def send_leave(k, leave):
        leave_out[k] = group_buf[k, 2 * N : 2 * N + 1] * leave + group_buf[k, N : 2 * N]
        leave_copy(k).start()

    def take_enter(k):
        @pl.when(is_first)
        def _():
            enter_in[k] = jnp.zeros((N, CHUNK), F32)

        @pl.when(jnp.logical_not(is_first))
        def _():
            enter_copy(k).wait_recv()

        @pl.when(jnp.logical_not(is_last))
        def _():
            send_enter(k, enter_in[k])

    def take_leave(k):
        @pl.when(is_last)
        def _():
            leave_in[k] = jnp.zeros((N, CHUNK), F32)

        @pl.when(jnp.logical_not(is_last))
        def _():
            leave_copy(k).wait_recv()

        @pl.when(jnp.logical_not(is_first))
        def _():
            send_leave(k, leave_in[k])

    def final_chunk(chunk):
        columns = pl.ds(pl.multiple_of(chunk * CHUNK, CHUNK), CHUNK)
        enter = carry_ref[chunk, :N]
        leave = carry_ref[chunk, N:]
        enter_high, enter_low = split_two(enter)
        leave_high, leave_low = split_two(leave)
        b, c = b_ref[...], c_ref[...]
        gw, xw = gw_ref[:, columns], xw_ref[:, columns]
        out = contract(jnp.concatenate([c, c], axis=1),
                       jnp.concatenate([enter_high, enter_low], axis=0), 1, 0)
        back = contract(jnp.concatenate([b, b], axis=1),
                        jnp.concatenate([leave_high, leave_low], axis=0), 1, 0)
        grad_ref[:, columns] = (
            within_ref[:, columns] + back * tail_ref[:, columns]
        ).astype(BF16)
        read_sum[...] += contract(jnp.concatenate([gw, gw], axis=1),
                                  jnp.concatenate([enter_high, enter_low], axis=1), 1, 1)
        write_sum[...] += contract(jnp.concatenate([xw, xw], axis=1),
                                   jnp.concatenate([leave_high, leave_low], axis=1), 1, 1)
        flow = flow_ref[:, columns] + gw.astype(F32) * out - xw.astype(F32) * back
        place = lax.broadcasted_iota(jnp.int32, (16, 256), 0)
        lanes = lax.broadcasted_iota(jnp.int32, (16, 256), 1)
        pick = jnp.where(lax.rem(lanes // P_SIZE, 2) == place, 1.0, 0.0).astype(BF16)
        sums = contract(pick, jnp.concatenate(split_two(flow), axis=1), 1, 1)
        for h in range(2):
            flowrow_ref[pl.ds(2 * chunk + h, 1), :] = sums[h : h + 1]
        end_state = pay_ref[chunk, 2 * N : 2 * N + 1] * enter + pay_ref[chunk, :N]
        ends_ref[pl.ds(chunk, 1), :] = jnp.sum(end_state * leave, axis=0, keepdims=True)

    def final_level(r, k, enter, leave):
        slot = r * CHUNKS + k
        mine = chunk_of(r, k, core)
        own, far = descend(is_core_late, pay_ref[mine], core_in[slot], enter, leave)
        back_out[slot, :N], back_out[slot, N:] = far
        back_copy(r, k).start()
        carry_ref[mine, :N], carry_ref[mine, N:] = own

    def group_join(k):
        pair_join(row, k)
        row_copy(k).wait_recv()
        early, late = ordered(is_row_late, pair_buf[row * CHUNKS + k], row_in[k])
        join(early, late, group_buf, k)

    def finish(k):
        own, far = descend(is_row_late, pair_buf[row * CHUNKS + k], row_in[k], enter_in[k],
                           leave_in[k])
        down_out[k, :N], down_out[k, N:] = far
        down_copy(k).start()
        final_level(row, k, *own)
        final_chunk(chunk_of(row, k, core))

    def down(k):
        down_copy(k).wait_recv()
        final_level(1 - row, k, down_in[k, :N], down_in[k, N:])
        final_chunk(chunk_of(1 - row, k, core))

    def take_back(r, k):
        chunk = chunk_of(r, k, 1 - core)
        back_copy(r, k).wait_recv()
        carry_ref[chunk] = back_in[r * CHUNKS + k]
        final_chunk(chunk)

    def stage(j, start, act):
        k = (j - start) // SPACING
        due = (j >= start) & (j < start + SPACING * CHUNKS) & (lax.rem(j - start, SPACING) == 0)

        @pl.when(due)
        def _():
            act(k)

    enter_start = JOIN_START + HOP * rank
    leave_start = JOIN_START + HOP * (ranks - 1 - rank)
    finish_start = jnp.maximum(enter_start, leave_start)
    down_start = finish_start + DOWN_LAG
    slots = JOIN_START + HOP * (ranks - 1) + DOWN_LAG + FAR_LAG + SPACING * CHUNKS

    @pl.loop(0, slots)
    def _(j):
        stage(j, JOIN_START, group_join)
        stage(j, enter_start, take_enter)
        stage(j, leave_start, take_leave)

        stage(j, finish_start, finish)
        stage(j, finish_start + NEAR_LAG, functools.partial(take_back, row))
        stage(j, down_start, down)
        stage(j, down_start + NEAR_LAG, functools.partial(take_back, 1 - row))

        @pl.when(j < WIDES)
        def _():
            block_wide(2 * lax.rem(j, CHUNKS) + j // CHUNKS)

        @pl.when(j == WIDES)
        def _():
            first = lax.broadcasted_iota(jnp.int32, (BLOCK, BLOCK), 0)
            second = lax.broadcasted_iota(jnp.int32, (BLOCK, BLOCK), 1)
            pairs = jnp.where(first <= second, pairs_ref[...], 0.0).astype(BF16)
            read_sum[...] += contract(pairs, b_ref[...], 0, 0)
            write_sum[...] += contract(pairs, c_ref[...], 1, 0)

    read_ref[...] = read_sum[...].astype(BF16)
    write_ref[...] = write_sum[...].astype(BF16)
    heads = lax.broadcasted_iota(jnp.int32, (HEADS, 32), 0)
    chunks = lax.broadcasted_iota(jnp.int32, (HEADS, 32), 1)
    pick = jnp.where(heads // 2 == chunks, 1.0, 0.0).astype(BF16)
    ends = sum(contract(pick, part, 1, 0) for part in split_three(ends_ref[...]))
    heads = lax.broadcasted_iota(jnp.int32, (HEADS, 128), 0)
    entries = lax.broadcasted_iota(jnp.int32, (HEADS, 128), 1)
    own_head = entries // P_SIZE == lax.rem(heads, 2)
    total = jnp.sum(jnp.where(own_head, ends, 0.0), axis=1, keepdims=True)
    flows = flowrow_ref[...] + outdot_ref[...]
    decay_ref[...] = total + sum(contract(part, lower_ones(), 1, 0) for part in split_three(flows))

    @pl.loop(0, CHUNKS)
    def _(k):
        for r in range(2):
            back_copy(r, k).wait_send()
            core_copy(r, k).wait_send()
        row_copy(k).wait_send()
        down_copy(k).wait_send()

        @pl.when(jnp.logical_not(is_last))
        def _():
            enter_copy(k).wait_send()

        @pl.when(jnp.logical_not(is_first))
        def _():
            leave_copy(k).wait_send()


def whole_call(x, g, b, c, rates, ranks):
    half, one = 2 * CHUNKS, CHUNKS

    def buffer(count, rows):
        return pltpu.VMEM((count, rows, CHUNK), F32)

    def wide(dtype):
        return pltpu.VMEM((BLOCK, WIDTH), dtype)

    def square(dtype):
        return pltpu.VMEM((BLOCK, BLOCK), dtype)

    def parts():
        return pltpu.VMEM((BLOCK, 128), BF16)

    def rows():
        return pltpu.VMEM((HEADS, BLOCK), F32)

    counts = [half, half] + [one] * 8 + [half, half]
    return pl.pallas_call(
        functools.partial(whole_kernel, ranks),
        out_shape=[
            pltpu.VMEM((BLOCK, WIDTH), BF16),
            pltpu.VMEM((BLOCK, N), BF16),
            pltpu.VMEM((BLOCK, N), BF16),
            pltpu.VMEM((HEADS, BLOCK), F32),
        ],
        in_specs=[pl.BlockSpec(memory_space=pltpu.HBM)] * 5,
        out_specs=[pl.BlockSpec(memory_space=pltpu.VMEM)] * 4,
        scratch_shapes=[
            wide(BF16), wide(BF16), parts(), parts(), rows(),
            wide(BF16), wide(BF16), wide(F32), wide(F32), wide(F32),
            rows(), rows(), rows(), pltpu.VMEM((32, CHUNK), F32),
            pltpu.VMEM((BLOCK, N), F32), pltpu.VMEM((BLOCK, N), F32),
            parts(), parts(), parts(), parts(), pltpu.VMEM((BLOCK, 128), F32),
            pltpu.VMEM((128, WIDE), jnp.int32),
            pltpu.VMEM((N, BLOCK), BF16), pltpu.VMEM((N, BLOCK), BF16),
            buffer(2 * half, PAY), buffer(2 * half, 2 * N),
            square(BF16), square(BF16), pltpu.VMEM((4, SUB, SUB), F32), square(F32),
            buffer(half, PAY), buffer(half, PAY), buffer(one, PAY), buffer(one, PAY),
            buffer(one, N), buffer(one, N), buffer(one, N), buffer(one, N),
            buffer(one, 2 * N), buffer(one, 2 * N), buffer(half, 2 * N), buffer(half, 2 * N),
            pltpu.SemaphoreType.DMA((WIDES,)), pltpu.SemaphoreType.DMA((WIDES,)),
            pltpu.SemaphoreType.DMA((3,)),
        ] + [pltpu.SemaphoreType.DMA((count,)) for count in counts],
        compiler_params=pltpu.CompilerParams(
            vmem_limit_bytes=VMEM_BYTES, collective_id=0, has_side_effects=True
        ),
    )(x, g, b, c, rates)


def store_kernel(*refs):
    sources, targets, sems = refs[:4], refs[4:8], refs[8]
    copies = [
        pltpu.make_async_copy(source, target, sems.at[index])
        for index, (source, target) in enumerate(zip(sources, targets))
    ]
    for copy in copies:
        copy.start()
    for copy in copies:
        copy.wait()


def store_call(results):
    return pl.pallas_call(
        store_kernel,
        out_shape=[jax.ShapeDtypeStruct(result.shape, result.dtype) for result in results],
        in_specs=[pl.BlockSpec(memory_space=pl.ANY)] * 4,
        out_specs=[pl.BlockSpec(memory_space=pl.ANY)] * 4,
        scratch_shapes=[pltpu.SemaphoreType.DMA((4,))],
        compiler_params=pltpu.CompilerParams(vmem_limit_bytes=COPY_BYTES),
    )(*results)


def body(inputs, write_vectors, read_vectors, log_decay, grad_out, *, seq_size):
    results = whole_call(
        inputs, grad_out, write_vectors, read_vectors, log_decay, seq_size // 4
    )
    return tuple(store_call(results))


def solution(mesh):
    rows = P(("grp", "seq"), None)
    columns = P(None, ("grp", "seq"))
    return jax.shard_map(
        functools.partial(body, seq_size=mesh.shape["seq"]),
        mesh=mesh,
        in_specs=(rows, rows, rows, columns, rows),
        out_specs=(rows, rows, rows, columns),
        check_vma=False,
    )
```

```python
import functools
import jax
import jax.numpy as jnp
from jax import lax
from jax.experimental import pallas as pl
from jax.experimental.pallas import tpu as pltpu
from jax.sharding import PartitionSpec as P

HEADS = 40
P_SIZE = 64
N = 128
BLOCK = 512
WIDTH = HEADS * P_SIZE
CHUNK = 128
WIDE = 256
CHUNKS = WIDTH // (4 * CHUNK)
WIDES = WIDTH // WIDE
SUB = 128
HALF = N // 2
PARTS = 2 * CHUNKS
PAY = 2 * HALF + 8
LOG2E = 1.4426950408889634
F32 = jnp.float32
BF16 = jnp.bfloat16
VMEM_BYTES = 53 * 1024 * 1024
COPY_BYTES = 1024 * 1024


def split_two(values):
    upper = values.astype(BF16)
    return upper, (values - upper.astype(F32)).astype(BF16)


def split_three(values):
    upper = values.astype(BF16)
    rest = values - upper.astype(F32)
    middle = rest.astype(BF16)
    return upper, middle, (rest - middle.astype(F32)).astype(BF16)


def contract(left, right, left_dim, right_dim):
    return lax.dot_general(
        left, right, (((left_dim,), (right_dim,)), ((), ())), preferred_element_type=F32
    )


def lower_ones():
    rows = lax.broadcasted_iota(jnp.int32, (BLOCK, BLOCK), 0)
    columns = lax.broadcasted_iota(jnp.int32, (BLOCK, BLOCK), 1)
    return jnp.where(rows >= columns, 1.0, 0.0).astype(BF16)


def parts_of(pay):
    return pay[:HALF], pay[HALF : 2 * HALF], pay[2 * HALF : 2 * HALF + 1]


def join(early, late, out_ref, index):
    early_s, early_r, early_d = parts_of(early)
    late_s, late_r, late_d = parts_of(late)
    out_ref[index, :HALF] = late_d * early_s + late_s
    out_ref[index, HALF : 2 * HALF] = early_r + early_d * late_r
    out_ref[index, 2 * HALF :] = jnp.broadcast_to(early_d * late_d, (8, CHUNK))


def ordered(is_late, mine, other):
    return jnp.where(is_late, other, mine), jnp.where(is_late, mine, other)


def descend(is_late, mine, other, enter, leave):
    early, late = ordered(is_late, mine, other)
    early_s, _, early_d = parts_of(early)
    _, late_r, late_d = parts_of(late)
    first_leave = late_r + late_d * leave
    second_enter = early_d * enter + early_s
    own = (jnp.where(is_late, second_enter, enter), jnp.where(is_late, leave, first_leave))
    far = (jnp.where(is_late, enter, second_enter), jnp.where(is_late, first_leave, leave))
    return own, far


JOIN_START = 0
SPACING = 1
HOP = 3
DOWN_LAG = 4
NEAR_LAG = 1


def three_lanes(values):
    lanes = lax.broadcasted_iota(jnp.int32, values.shape, 1)
    upper, middle, rest = [part.astype(F32) for part in split_three(values)]
    picked = jnp.where(lanes < HEADS, upper, jnp.where(lanes < 2 * HEADS, middle, rest))
    return jnp.where(lanes < 3 * HEADS, picked, 0.0).astype(BF16)


def lane_pick(values, lane):
    index = jnp.full(values.shape, lane, jnp.int32)
    return jnp.take_along_axis(values, index, axis=1, mode="promise_in_bounds")


def whole_kernel(ranks, x_hbm, g_hbm, b_hbm, c_hbm, rate_hbm,
                 grad_ref, write_ref, read_ref, decay_ref,
                 x_ref, g_ref, b_ref, c_ref, rate_ref,
                 xw_ref, gw_ref, tail_ref, within_ref, flow_ref,
                 cumrow_ref, outdot_ref, flowrow_ref, ends_ref,
                 read_sum, write_sum, growth_parts, tail_parts, one_parts, two_parts, cum_ref,
                 heads_ref, b_turned, c_turned, pay_ref, carry_ref,
                 cross_ref, turned_ref, diag_ref, pairs_ref, core_in, pair_buf, row_in, group_buf,
                 enter_in, enter_out, leave_in, leave_out, down_out, down_in, back_out, back_in,
                 x_sem, g_sem, small_sem,
                 core_send, core_recv, row_send, row_recv, enter_send, enter_recv, leave_send,
                 leave_recv, down_send, down_recv, back_send, back_recv):
    me = lax.axis_index("seq")
    core = lax.rem(me, 2)
    row = lax.rem(me // 2, 2)
    rank = me // 4
    core_peer = me + 1 - 2 * core
    row_peer = me + 2 - 4 * row
    is_first, is_last = rank == 0, rank == ranks - 1

    def remote(source, target, send, recv, peer):
        return pltpu.make_async_remote_copy(
            src_ref=source, dst_ref=target, send_sem=send, recv_sem=recv,
            device_id={"seq": peer}, device_id_type=pl.DeviceIdType.MESH,
        )

    def chunk_of(r, k, q):
        return 4 * k + 2 * r + q

    def core_copy(r, k):
        slot = r * CHUNKS + k
        mine = pay_ref.at[pl.ds(2 * chunk_of(r, k, 1 - core), 2)]
        return remote(mine, core_in.at[pl.ds(2 * slot, 2)], core_send.at[slot],
                      core_recv.at[slot], core_peer)

    def row_copy(m):
        return remote(pair_buf.at[(1 - row) * PARTS + m], row_in.at[m], row_send.at[m],
                      row_recv.at[m], row_peer)

    def enter_copy(m):
        return remote(enter_out.at[m], enter_in.at[m], enter_send.at[m], enter_recv.at[m], me + 4)

    def leave_copy(m):
        return remote(leave_out.at[m], leave_in.at[m], leave_send.at[m], leave_recv.at[m], me - 4)

    def down_copy(m):
        return remote(down_out.at[m], down_in.at[m], down_send.at[m], down_recv.at[m], row_peer)

    def back_copy(r, m):
        slot = r * PARTS + m
        return remote(back_out.at[slot], back_in.at[slot], back_send.at[slot], back_recv.at[slot],
                      core_peer)

    def part_of(r, m, q):
        return 2 * chunk_of(r, m // 2, q) + lax.rem(m, 2)

    def wide_of(step):
        return 2 * lax.rem(step, CHUNKS) + jnp.where(step < CHUNKS, 1 - row, row)

    def columns_of(w):
        return pl.ds(pl.multiple_of(w * WIDE, WIDE), WIDE)

    def load(w):
        return (pltpu.make_async_copy(x_hbm.at[:, columns_of(w)], x_ref.at[:, columns_of(w)],
                                      x_sem.at[w]),
                pltpu.make_async_copy(g_hbm.at[:, columns_of(w)], g_ref.at[:, columns_of(w)],
                                      g_sem.at[w]))

    small = [pltpu.make_async_copy(source, target, small_sem.at[index])
             for index, (source, target) in enumerate(
                 ((rate_hbm, rate_ref), (b_hbm, b_ref), (c_hbm, c_ref)))]
    for copy in small:
        copy.start()

    @pl.loop(0, WIDES)
    def _(step):
        for copy in load(wide_of(step)):
            copy.start()

    barrier = pltpu.get_barrier_semaphore()

    def greet(peer):
        pl.semaphore_signal(barrier, inc=1, device_id={"seq": peer},
                            device_id_type=pl.DeviceIdType.MESH)

    greet(core_peer)
    greet(row_peer)

    @pl.when(jnp.logical_not(is_first))
    def _():
        greet(me - 4)

    @pl.when(jnp.logical_not(is_last))
    def _():
        greet(me + 4)

    source = lax.broadcasted_iota(jnp.int32, (128, WIDE), 0)
    target = lax.broadcasted_iota(jnp.int32, (128, WIDE), 1)
    head = source - jnp.where(source >= HEADS, HEADS, 0) - jnp.where(source >= 2 * HEADS, HEADS, 0)
    head = jnp.where(source < 3 * HEADS, head, 4 * HEADS)
    heads_ref[...] = head - target // P_SIZE

    small[0].wait()
    lower = lower_ones()
    rates = rate_ref[...] * LOG2E
    padded = jnp.concatenate([rates, rates, rates, jnp.zeros((8, BLOCK), F32)], axis=0)
    cum = sum(contract(lower, part, 1, 1) for part in split_three(padded))
    growth_parts[...] = three_lanes(jnp.exp2(cum))
    tail_parts[...] = three_lanes(jnp.exp2(cum[BLOCK - 1 :] - cum))
    for copy in small[1:]:
        copy.wait()
    b_turned[...] = b_ref[...].astype(F32).T.astype(BF16)
    c_turned[...] = c_ref[...].astype(F32).T.astype(BF16)
    cum_ref[...] = cum

    def local_wide(w):
        columns = columns_of(w)
        spread = jnp.where(heads_ref[...] == 4 * w, 1.0, 0.0).astype(BF16)
        growth = contract(growth_parts[...], spread, 1, 0)
        tail = contract(tail_parts[...], spread, 1, 0)
        x_weighted = (x_ref[:, columns].astype(F32) * tail).astype(BF16)
        g_weighted = (g_ref[:, columns].astype(F32) * growth).astype(BF16)
        xw_ref[:, columns] = x_weighted
        gw_ref[:, columns] = g_weighted
        tail_ref[:, columns] = tail
        state = contract(b_turned[...], x_weighted, 1, 0)
        adjoint = contract(c_turned[...], g_weighted, 1, 0)
        decay = jnp.broadcast_to(growth[BLOCK - 1 :], (8, WIDE))
        for q in range(2):
            lanes = slice(q * CHUNK, (q + 1) * CHUNK)
            for part in range(2):
                rows = slice(part * HALF, (part + 1) * HALF)
                mine = 2 * (2 * w + q) + part
                pay_ref[mine, :HALF] = state[rows, lanes]
                pay_ref[mine, HALF : 2 * HALF] = adjoint[rows, lanes]
                pay_ref[mine, 2 * HALF :] = decay[:, lanes]

    is_core_late, is_row_late = core == 1, row == 1

    def pair_join(r, m):
        slot = r * PARTS + m
        early, late = ordered(is_core_late, pay_ref[part_of(r, m, core)], core_in[slot])
        join(early, late, pair_buf, slot)

    chain_peers = jnp.where(is_first, 0, 1) + jnp.where(is_last, 0, 1)
    pl.semaphore_wait(barrier, 2 + chain_peers)

    @pl.loop(0, WIDES)
    def _(step):
        w = wide_of(step)
        for copy in load(w):
            copy.wait()
        local_wide(w)
        core_copy(lax.rem(w, 2), w // 2).start()

        @pl.when((step >= 1) & (step <= CHUNKS))
        def _():
            core_copy(1 - row, step - 1).wait_recv()
            for part in range(2):
                pair_join(1 - row, 2 * step - 2 + part)
                row_copy(2 * step - 2 + part).start()

    one_parts[...] = three_lanes(jnp.exp2(-jnp.abs(cum - cum[2 * SUB - 1 : 2 * SUB])))
    two_parts[...] = three_lanes(jnp.exp2(-jnp.abs(cum - jnp.concatenate(
        [jnp.broadcast_to(cum[at : at + 1], (2 * SUB, 128)) for at in (SUB - 1, 3 * SUB - 1)],
        axis=0))))
    cumrow_ref[...] = sum(contract(part, lower, 1, 1) for part in split_three(rates))
    scores = contract(b_ref[...], c_ref[...], 1, 1)
    cross_ref[...] = scores.astype(BF16)
    turned_ref[...] = contract(c_ref[...], b_ref[...], 1, 1).astype(BF16)
    upper = lax.broadcasted_iota(jnp.int32, (SUB, SUB), 0) <= lax.broadcasted_iota(
        jnp.int32, (SUB, SUB), 1)
    for sub in range(4):
        rows = slice(sub * SUB, (sub + 1) * SUB)
        diag_ref[sub] = jnp.where(upper, scores[rows, rows], 0.0)
    pairs_ref[...] = jnp.zeros_like(pairs_ref)
    ends_ref[...] = jnp.zeros_like(ends_ref)
    read_sum[...] = jnp.zeros_like(read_sum)
    write_sum[...] = jnp.zeros_like(write_sum)

    def block_wide(w):
        columns = columns_of(w)
        spread = jnp.where(heads_ref[...] == 4 * w, 1.0, 0.0).astype(BF16)
        one = contract(one_parts[...], spread, 1, 0)
        two = contract(two_parts[...], spread, 1, 0)
        x, g = x_ref[:, columns], g_ref[:, columns]
        half = 2 * SUB
        x_one = (x[:half].astype(F32) * one[:half]).astype(BF16)
        g_one = (g[half:].astype(F32) * one[half:]).astype(BF16)
        pairs_ref[:half, half:] += contract(x_one, g_one, 1, 1)
        back_one = contract(cross_ref[:half, half:], g_one, 1, 0)
        out_one = contract(turned_ref[half:, :half], x_one, 1, 0)
        flow_one = [x_one.astype(F32) * back_one, g_one.astype(F32) * out_one]
        lanes = lax.broadcasted_iota(jnp.int32, (SUB, 128), 1)
        zero = jnp.zeros((), BF16)
        out_dots = [[] for _ in range(4)]
        cum_heads = [cumrow_ref[pl.ds(4 * w + h, 1), :] for h in range(4)]
        for side in range(2):
            early = slice(side * half, side * half + SUB)
            late = slice(side * half + SUB, (side + 1) * half)
            x_two = (x[early].astype(F32) * two[early]).astype(BF16)
            g_two = (g[late].astype(F32) * two[late]).astype(BF16)
            pairs_ref[early, late] += contract(x_two, g_two, 1, 1)
            back_two = contract(cross_ref[early, late], g_two, 1, 0)
            out_two = contract(turned_ref[late, early], x_two, 1, 0)
            flow_two = [-(x_two.astype(F32) * back_two), g_two.astype(F32) * out_two]
            for part, rows in enumerate((early, late)):
                local = slice(part * SUB, (part + 1) * SUB)
                if side == 0:
                    flow = flow_two[part] - flow_one[0][local]
                    within = one[rows] * back_one[local]
                    if part == 0:
                        within = within + two[rows] * back_two
                else:
                    flow = flow_two[part] + flow_one[1][local]
                    within = two[rows] * back_two if part == 0 else None
                sub = 2 * side + part
                scores = diag_ref[sub]
                scores = jnp.concatenate([scores, scores], axis=1)
                added = pairs_ref[rows, rows]
                for pair in range(2):
                    place = slice(pair * 128, (pair + 1) * 128)
                    xs, gs = x[rows, place], g[rows, place]
                    g_split = jnp.concatenate(
                        [jnp.where(lanes < P_SIZE, gs, zero), jnp.where(lanes >= P_SIZE, gs, zero)],
                        axis=0)
                    products = contract(xs, g_split, 1, 1)
                    gap = jnp.concatenate(
                        [lane_pick(cum_ref[rows, :], 4 * w + 2 * pair + h) for h in range(2)],
                        axis=1)
                    cum_rows = jnp.concatenate(
                        [cum_heads[2 * pair + h][:, rows] for h in range(2)],
                        axis=1)
                    decay = jnp.exp2(jnp.minimum(cum_rows - gap, 0.0))
                    decayed = products * decay
                    added = added + decayed[:, :SUB] + decayed[:, SUB:]
                    mixing = (scores * decay).astype(BF16)
                    out_dot = jnp.sum(mixing.astype(F32) * products, axis=0, keepdims=True)
                    for h in range(2):
                        out_dots[2 * pair + h].append(out_dot[:, h * SUB : (h + 1) * SUB])
                    back = contract(mixing, g_split, 1, 0)
                    at = pl.ds(pl.multiple_of(w * WIDE + pair * 128, 128), 128)
                    within_ref[rows, at] = back if within is None else within[:, place] + back
                    flow_ref[rows, at] = flow[:, place] - xs.astype(F32) * back
                pairs_ref[rows, rows] = added
        for h in range(4):
            outdot_ref[pl.ds(4 * w + h, 1), :] = jnp.concatenate(out_dots[h], axis=1)

    def send_enter(m, enter):
        enter_out[m] = group_buf[m, 2 * HALF : 2 * HALF + 1] * enter + group_buf[m, :HALF]
        enter_copy(m).start()

    def send_leave(m, leave):
        leave_out[m] = group_buf[m, 2 * HALF : 2 * HALF + 1] * leave + group_buf[m, HALF : 2 * HALF]
        leave_copy(m).start()

    def take_enter(m):
        @pl.when(is_first)
        def _():
            enter_in[m] = jnp.zeros((HALF, CHUNK), F32)

        @pl.when(jnp.logical_not(is_first))
        def _():
            enter_copy(m).wait_recv()

        @pl.when(jnp.logical_not(is_last))
        def _():
            send_enter(m, enter_in[m])

    def take_leave(m):
        @pl.when(is_last)
        def _():
            leave_in[m] = jnp.zeros((HALF, CHUNK), F32)

        @pl.when(jnp.logical_not(is_last))
        def _():
            leave_copy(m).wait_recv()

        @pl.when(jnp.logical_not(is_first))
        def _():
            send_leave(m, leave_in[m])

    def final_chunk(chunk):
        columns = pl.ds(pl.multiple_of(chunk * CHUNK, CHUNK), CHUNK)
        enter = jnp.concatenate([carry_ref[2 * chunk + part, :HALF] for part in range(2)], axis=0)
        leave = jnp.concatenate([carry_ref[2 * chunk + part, HALF:] for part in range(2)], axis=0)
        enter_high, enter_low = split_two(enter)
        leave_high, leave_low = split_two(leave)
        b, c = b_ref[...], c_ref[...]
        gw, xw = gw_ref[:, columns], xw_ref[:, columns]
        out = contract(jnp.concatenate([c, c], axis=1),
                       jnp.concatenate([enter_high, enter_low], axis=0), 1, 0)
        back = contract(jnp.concatenate([b, b], axis=1),
                        jnp.concatenate([leave_high, leave_low], axis=0), 1, 0)
        grad_ref[:, columns] = (
            within_ref[:, columns] + back * tail_ref[:, columns]
        ).astype(BF16)
        read_sum[...] += contract(jnp.concatenate([gw, gw], axis=1),
                                  jnp.concatenate([enter_high, enter_low], axis=1), 1, 1)
        write_sum[...] += contract(jnp.concatenate([xw, xw], axis=1),
                                   jnp.concatenate([leave_high, leave_low], axis=1), 1, 1)
        flow = flow_ref[:, columns] + gw.astype(F32) * out - xw.astype(F32) * back
        place = lax.broadcasted_iota(jnp.int32, (16, 256), 0)
        lanes = lax.broadcasted_iota(jnp.int32, (16, 256), 1)
        pick = jnp.where(lax.rem(lanes // P_SIZE, 2) == place, 1.0, 0.0).astype(BF16)
        sums = contract(pick, jnp.concatenate(split_two(flow), axis=1), 1, 1)
        for h in range(2):
            flowrow_ref[pl.ds(2 * chunk + h, 1), :] = sums[h : h + 1]
        local = jnp.concatenate([pay_ref[2 * chunk + part, :HALF] for part in range(2)], axis=0)
        end_state = pay_ref[2 * chunk, 2 * HALF : 2 * HALF + 1] * enter + local
        ends_ref[pl.ds(chunk, 1), :] = jnp.sum(end_state * leave, axis=0, keepdims=True)

    def final_level(r, m, enter, leave):
        slot = r * PARTS + m
        mine = part_of(r, m, core)
        own, far = descend(is_core_late, pay_ref[mine], core_in[slot], enter, leave)
        back_out[slot, :HALF], back_out[slot, HALF:] = far
        back_copy(r, m).start()
        carry_ref[mine, :HALF], carry_ref[mine, HALF:] = own

        @pl.when(lax.rem(m, 2) == 1)
        def _():
            final_chunk(chunk_of(r, m // 2, core))

    def group_join(m):
        @pl.when(lax.rem(m, 2) == 0)
        def _():
            core_copy(row, m // 2).wait_recv()

        pair_join(row, m)
        row_copy(m).wait_recv()
        early, late = ordered(is_row_late, pair_buf[row * PARTS + m], row_in[m])
        join(early, late, group_buf, m)

    def finish(m):
        own, far = descend(is_row_late, pair_buf[row * PARTS + m], row_in[m], enter_in[m],
                           leave_in[m])
        down_out[m, :HALF], down_out[m, HALF:] = far
        down_copy(m).start()
        final_level(row, m, *own)

    def down(m):
        down_copy(m).wait_recv()
        final_level(1 - row, m, down_in[m, :HALF], down_in[m, HALF:])

    def take_back(r, m):
        back_copy(r, m).wait_recv()
        carry_ref[part_of(r, m, 1 - core)] = back_in[r * PARTS + m]

        @pl.when(lax.rem(m, 2) == 1)
        def _():
            final_chunk(chunk_of(r, m // 2, 1 - core))

    def stage(j, start, act):
        m = (j - start) // SPACING
        due = (j >= start) & (j < start + SPACING * PARTS) & (lax.rem(j - start, SPACING) == 0)

        @pl.when(due)
        def _():
            act(m)

    enter_start = JOIN_START + HOP * rank
    leave_start = JOIN_START + HOP * (ranks - 1 - rank)
    finish_start = jnp.maximum(enter_start, leave_start)
    down_start = finish_start + DOWN_LAG
    slots = JOIN_START + HOP * (ranks - 1) + DOWN_LAG + NEAR_LAG + SPACING * PARTS

    @pl.loop(0, slots)
    def _(j):
        stage(j, JOIN_START, group_join)
        stage(j, enter_start, take_enter)
        stage(j, leave_start, take_leave)
        stage(j, finish_start, finish)
        stage(j, finish_start + NEAR_LAG, functools.partial(take_back, row))
        stage(j, down_start, down)
        stage(j, down_start + NEAR_LAG, functools.partial(take_back, 1 - row))

        @pl.when(j < WIDES)
        def _():
            block_wide(2 * lax.rem(j, CHUNKS) + j // CHUNKS)

        @pl.when(j == WIDES)
        def _():
            first = lax.broadcasted_iota(jnp.int32, (BLOCK, BLOCK), 0)
            second = lax.broadcasted_iota(jnp.int32, (BLOCK, BLOCK), 1)
            pairs = jnp.where(first <= second, pairs_ref[...], 0.0).astype(BF16)
            read_sum[...] += contract(pairs, b_ref[...], 0, 0)
            write_sum[...] += contract(pairs, c_ref[...], 1, 0)

    read_ref[...] = read_sum[...].astype(BF16)
    write_ref[...] = write_sum[...].astype(BF16)
    heads = lax.broadcasted_iota(jnp.int32, (HEADS, 32), 0)
    chunks = lax.broadcasted_iota(jnp.int32, (HEADS, 32), 1)
    pick = jnp.where(heads // 2 == chunks, 1.0, 0.0).astype(BF16)
    ends = sum(contract(pick, part, 1, 0) for part in split_three(ends_ref[...]))
    heads = lax.broadcasted_iota(jnp.int32, (HEADS, 128), 0)
    entries = lax.broadcasted_iota(jnp.int32, (HEADS, 128), 1)
    own_head = entries // P_SIZE == lax.rem(heads, 2)
    total = jnp.sum(jnp.where(own_head, ends, 0.0), axis=1, keepdims=True)
    flows = flowrow_ref[...] + outdot_ref[...]
    decay_ref[...] = total + sum(contract(part, lower_ones(), 1, 0) for part in split_three(flows))

    @pl.loop(0, CHUNKS)
    def _(k):
        for r in range(2):
            core_copy(r, k).wait_send()

    @pl.loop(0, PARTS)
    def _(m):
        for r in range(2):
            back_copy(r, m).wait_send()
        row_copy(m).wait_send()
        down_copy(m).wait_send()

        @pl.when(jnp.logical_not(is_last))
        def _():
            enter_copy(m).wait_send()

        @pl.when(jnp.logical_not(is_first))
        def _():
            leave_copy(m).wait_send()


def whole_call(x, g, b, c, rates, ranks):
    half, one = 2 * PARTS, PARTS

    def buffer(count, rows):
        return pltpu.VMEM((count, rows, CHUNK), F32)

    def wide(dtype):
        return pltpu.VMEM((BLOCK, WIDTH), dtype)

    def square(dtype):
        return pltpu.VMEM((BLOCK, BLOCK), dtype)

    def parts():
        return pltpu.VMEM((BLOCK, 128), BF16)

    def rows():
        return pltpu.VMEM((HEADS, BLOCK), F32)

    counts = [one, one] + [one] * 8 + [half, half]
    return pl.pallas_call(
        functools.partial(whole_kernel, ranks),
        out_shape=[
            pltpu.VMEM((BLOCK, WIDTH), BF16),
            pltpu.VMEM((BLOCK, N), BF16),
            pltpu.VMEM((BLOCK, N), BF16),
            pltpu.VMEM((HEADS, BLOCK), F32),
        ],
        in_specs=[pl.BlockSpec(memory_space=pltpu.HBM)] * 5,
        out_specs=[pl.BlockSpec(memory_space=pltpu.VMEM)] * 4,
        scratch_shapes=[
            wide(BF16), wide(BF16), parts(), parts(), rows(),
            wide(BF16), wide(BF16), wide(F32), wide(F32), wide(F32),
            rows(), rows(), rows(), pltpu.VMEM((32, CHUNK), F32),
            pltpu.VMEM((BLOCK, N), F32), pltpu.VMEM((BLOCK, N), F32),
            parts(), parts(), parts(), parts(), pltpu.VMEM((BLOCK, 128), F32),
            pltpu.VMEM((128, WIDE), jnp.int32),
            pltpu.VMEM((N, BLOCK), BF16), pltpu.VMEM((N, BLOCK), BF16),
            buffer(2 * half, PAY), buffer(2 * half, 2 * HALF),
            square(BF16), square(BF16), pltpu.VMEM((4, SUB, SUB), F32), square(F32),
            buffer(half, PAY), buffer(half, PAY), buffer(one, PAY), buffer(one, PAY),
            buffer(one, HALF), buffer(one, HALF), buffer(one, HALF), buffer(one, HALF),
            buffer(one, 2 * HALF), buffer(one, 2 * HALF), buffer(half, 2 * HALF),
            buffer(half, 2 * HALF),
            pltpu.SemaphoreType.DMA((WIDES,)), pltpu.SemaphoreType.DMA((WIDES,)),
            pltpu.SemaphoreType.DMA((3,)),
        ] + [pltpu.SemaphoreType.DMA((count,)) for count in counts],
        compiler_params=pltpu.CompilerParams(
            vmem_limit_bytes=VMEM_BYTES, collective_id=0, has_side_effects=True
        ),
    )(x, g, b, c, rates)


def store_kernel(*refs):
    sources, targets, sems = refs[:4], refs[4:8], refs[8]
    copies = [
        pltpu.make_async_copy(source, target, sems.at[index])
        for index, (source, target) in enumerate(zip(sources, targets))
    ]
    for copy in copies:
        copy.start()
    for copy in copies:
        copy.wait()


def store_call(results):
    return pl.pallas_call(
        store_kernel,
        out_shape=[jax.ShapeDtypeStruct(result.shape, result.dtype) for result in results],
        in_specs=[pl.BlockSpec(memory_space=pl.ANY)] * 4,
        out_specs=[pl.BlockSpec(memory_space=pl.ANY)] * 4,
        scratch_shapes=[pltpu.SemaphoreType.DMA((4,))],
        compiler_params=pltpu.CompilerParams(vmem_limit_bytes=COPY_BYTES),
    )(*results)


def body(inputs, write_vectors, read_vectors, log_decay, grad_out, *, seq_size):
    results = whole_call(
        inputs, grad_out, write_vectors, read_vectors, log_decay, seq_size // 4
    )
    return tuple(store_call(results))


def solution(mesh):
    rows = P(("grp", "seq"), None)
    columns = P(None, ("grp", "seq"))
    return jax.shard_map(
        functools.partial(body, seq_size=mesh.shape["seq"]),
        mesh=mesh,
        in_specs=(rows, rows, rows, columns, rows),
        out_specs=(rows, rows, rows, columns),
        check_vma=False,
    )
```

```python
import functools
import jax
import jax.numpy as jnp
from jax import lax
from jax.experimental import pallas as pl
from jax.experimental.pallas import tpu as pltpu
from jax.sharding import PartitionSpec as P

HEADS = 40
P_SIZE = 64
N = 128
BLOCK = 512
WIDTH = HEADS * P_SIZE
CHUNK = 128
WIDE = 256
CHUNKS = WIDTH // (4 * CHUNK)
WIDES = WIDTH // WIDE
SUB = 128
HALF = N // 2
PARTS = 2 * CHUNKS
PAY = 2 * HALF + 8
SENT = 2 * HALF + 1
LOG2E = 1.4426950408889634
F32 = jnp.float32
BF16 = jnp.bfloat16
VMEM_BYTES = 53 * 1024 * 1024
COPY_BYTES = 1024 * 1024


def split_two(values):
    upper = values.astype(BF16)
    return upper, (values - upper.astype(F32)).astype(BF16)


def split_three(values):
    upper = values.astype(BF16)
    rest = values - upper.astype(F32)
    middle = rest.astype(BF16)
    return upper, middle, (rest - middle.astype(F32)).astype(BF16)


def contract(left, right, left_dim, right_dim):
    return lax.dot_general(
        left, right, (((left_dim,), (right_dim,)), ((), ())), preferred_element_type=F32
    )


def lower_ones():
    rows = lax.broadcasted_iota(jnp.int32, (BLOCK, BLOCK), 0)
    columns = lax.broadcasted_iota(jnp.int32, (BLOCK, BLOCK), 1)
    return jnp.where(rows >= columns, 1.0, 0.0).astype(BF16)


def parts_of(pay):
    return pay[:HALF], pay[HALF : 2 * HALF], pay[2 * HALF : 2 * HALF + 1]


def join(early, late, out_ref, index):
    early_s, early_r, early_d = parts_of(early)
    late_s, late_r, late_d = parts_of(late)
    out_ref[index, :HALF] = late_d * early_s + late_s
    out_ref[index, HALF : 2 * HALF] = early_r + early_d * late_r
    out_ref[index, 2 * HALF :] = jnp.broadcast_to(early_d * late_d, (8, CHUNK))


def ordered(is_late, mine, other):
    return jnp.where(is_late, other, mine), jnp.where(is_late, mine, other)


def descend(is_late, mine, other, enter, leave):
    early, late = ordered(is_late, mine, other)
    early_s, _, early_d = parts_of(early)
    _, late_r, late_d = parts_of(late)
    first_leave = late_r + late_d * leave
    second_enter = early_d * enter + early_s
    own = (jnp.where(is_late, second_enter, enter), jnp.where(is_late, leave, first_leave))
    far = (jnp.where(is_late, enter, second_enter), jnp.where(is_late, first_leave, leave))
    return own, far


JOIN_START = 0
SPACING = 1
HOP = 3
DOWN_LAG = 4
NEAR_LAG = 1


def three_lanes(values):
    lanes = lax.broadcasted_iota(jnp.int32, values.shape, 1)
    upper, middle, rest = [part.astype(F32) for part in split_three(values)]
    picked = jnp.where(lanes < HEADS, upper, jnp.where(lanes < 2 * HEADS, middle, rest))
    return jnp.where(lanes < 3 * HEADS, picked, 0.0).astype(BF16)


def three_sums(values, square, square_dim):
    stacked = jnp.concatenate(
        [part.astype(F32) for part in split_three(values)] + [jnp.zeros((8, BLOCK), F32)], axis=0
    ).astype(BF16)
    sums = contract(stacked, square, 1, square_dim)
    return sums[:HEADS] + sums[HEADS : 2 * HEADS] + sums[2 * HEADS : 3 * HEADS]


def lane_pick(values, lane):
    index = jnp.full(values.shape, lane, jnp.int32)
    return jnp.take_along_axis(values, index, axis=1, mode="promise_in_bounds")


def whole_kernel(ranks, x_hbm, g_hbm, b_hbm, c_hbm, rate_hbm,
                 grad_ref, write_ref, read_ref, decay_ref,
                 x_ref, g_ref, b_ref, c_ref, rate_ref,
                 xw_ref, gw_ref, tail_ref, within_ref, flow_ref,
                 cumrow_ref, outdot_ref, flowrow_ref, ends_ref,
                 read_sum, write_sum, growth_parts, tail_parts, one_parts, two_parts, cum_ref,
                 heads_ref, b_turned, c_turned, pay_ref, carry_ref,
                 lower_ref, cross_ref, turned_ref, diag_ref, pairs_ref, core_in, pair_buf, row_in, group_buf,
                 enter_in, enter_out, leave_in, leave_out, down_out, down_in, back_out, back_in,
                 x_sem, g_sem, small_sem,
                 core_send, core_recv, row_send, row_recv, enter_send, enter_recv, leave_send,
                 leave_recv, down_send, down_recv, back_send, back_recv):
    me = lax.axis_index("seq")
    core = lax.rem(me, 2)
    row = lax.rem(me // 2, 2)
    rank = me // 4
    core_peer = me + 1 - 2 * core
    row_peer = me + 2 - 4 * row
    is_first, is_last = rank == 0, rank == ranks - 1

    def remote(source, target, send, recv, peer):
        return pltpu.make_async_remote_copy(
            src_ref=source, dst_ref=target, send_sem=send, recv_sem=recv,
            device_id={"seq": peer}, device_id_type=pl.DeviceIdType.MESH,
        )

    def chunk_of(r, k, q):
        return 4 * k + 2 * r + q

    def core_copy(r, k):
        slot = r * CHUNKS + k
        mine = pay_ref.at[pl.ds(2 * chunk_of(r, k, 1 - core), 2)]
        return remote(mine, core_in.at[pl.ds(2 * slot, 2)], core_send.at[slot],
                      core_recv.at[slot], core_peer)

    def row_copy(m):
        sent = pl.ds(0, SENT)
        return remote(pair_buf.at[(1 - row) * PARTS + m, sent], row_in.at[m, sent],
                      row_send.at[m], row_recv.at[m], row_peer)

    def enter_copy(m):
        return remote(enter_out.at[m], enter_in.at[m], enter_send.at[m], enter_recv.at[m], me + 4)

    def leave_copy(m):
        return remote(leave_out.at[m], leave_in.at[m], leave_send.at[m], leave_recv.at[m], me - 4)

    def down_copy(m):
        return remote(down_out.at[m], down_in.at[m], down_send.at[m], down_recv.at[m], row_peer)

    def back_copy(r, m):
        slot = r * PARTS + m
        return remote(back_out.at[slot], back_in.at[slot], back_send.at[slot], back_recv.at[slot],
                      core_peer)

    def part_of(r, m, q):
        return 2 * chunk_of(r, m // 2, q) + lax.rem(m, 2)

    def wide_of(step):
        return 2 * lax.rem(step, CHUNKS) + jnp.where(step < CHUNKS, 1 - row, row)

    def columns_of(w):
        return pl.ds(pl.multiple_of(w * WIDE, WIDE), WIDE)

    def load(w):
        return (pltpu.make_async_copy(x_hbm.at[:, columns_of(w)], x_ref.at[:, columns_of(w)],
                                      x_sem.at[w]),
                pltpu.make_async_copy(g_hbm.at[:, columns_of(w)], g_ref.at[:, columns_of(w)],
                                      g_sem.at[w]))

    small = [pltpu.make_async_copy(source, target, small_sem.at[index])
             for index, (source, target) in enumerate(
                 ((rate_hbm, rate_ref), (b_hbm, b_ref), (c_hbm, c_ref)))]
    for copy in small:
        copy.start()

    @pl.loop(0, WIDES)
    def _(step):
        for copy in load(wide_of(step)):
            copy.start()

    barrier = pltpu.get_barrier_semaphore()

    def greet(peer):
        pl.semaphore_signal(barrier, inc=1, device_id={"seq": peer},
                            device_id_type=pl.DeviceIdType.MESH)

    greet(core_peer)
    greet(row_peer)

    @pl.when(jnp.logical_not(is_first))
    def _():
        greet(me - 4)

    @pl.when(jnp.logical_not(is_last))
    def _():
        greet(me + 4)

    source = lax.broadcasted_iota(jnp.int32, (128, WIDE), 0)
    target = lax.broadcasted_iota(jnp.int32, (128, WIDE), 1)
    head = source - jnp.where(source >= HEADS, HEADS, 0) - jnp.where(source >= 2 * HEADS, HEADS, 0)
    head = jnp.where(source < 3 * HEADS, head, 4 * HEADS)
    heads_ref[...] = head - target // P_SIZE

    lower_ref[...] = lower_ones()
    small[0].wait()
    cum_rows = three_sums(rate_ref[...] * LOG2E, lower_ref[...], 1)
    cumrow_ref[...] = cum_rows
    cum = jnp.concatenate([cum_rows, cum_rows, cum_rows, jnp.zeros((8, BLOCK), F32)], axis=0).T
    growth_parts[...] = three_lanes(jnp.exp2(cum))
    tail_parts[...] = three_lanes(jnp.exp2(cum[BLOCK - 1 :] - cum))
    for copy in small[1:]:
        copy.wait()
    b_turned[...] = b_ref[...].astype(F32).T.astype(BF16)
    c_turned[...] = c_ref[...].astype(F32).T.astype(BF16)
    cum_ref[...] = cum

    def local_wide(w):
        columns = columns_of(w)
        spread = jnp.where(heads_ref[...] == 4 * w, 1.0, 0.0).astype(BF16)
        growth = contract(growth_parts[...], spread, 1, 0)
        tail = contract(tail_parts[...], spread, 1, 0)
        x_weighted = (x_ref[:, columns].astype(F32) * tail).astype(BF16)
        g_weighted = (g_ref[:, columns].astype(F32) * growth).astype(BF16)
        xw_ref[:, columns] = x_weighted
        gw_ref[:, columns] = g_weighted
        tail_ref[:, columns] = tail
        state = contract(b_turned[...], x_weighted, 1, 0)
        adjoint = contract(c_turned[...], g_weighted, 1, 0)
        decay = jnp.broadcast_to(growth[BLOCK - 1 :], (8, WIDE))
        for q in range(2):
            lanes = slice(q * CHUNK, (q + 1) * CHUNK)
            for part in range(2):
                rows = slice(part * HALF, (part + 1) * HALF)
                mine = 2 * (2 * w + q) + part
                pay_ref[mine, :HALF] = state[rows, lanes]
                pay_ref[mine, HALF : 2 * HALF] = adjoint[rows, lanes]
                pay_ref[mine, 2 * HALF :] = decay[:, lanes]

    is_core_late, is_row_late = core == 1, row == 1

    def pair_join(r, m):
        slot = r * PARTS + m
        early, late = ordered(is_core_late, pay_ref[part_of(r, m, core)], core_in[slot])
        join(early, late, pair_buf, slot)

    chain_peers = jnp.where(is_first, 0, 1) + jnp.where(is_last, 0, 1)
    pl.semaphore_wait(barrier, 2 + chain_peers)

    @pl.loop(0, WIDES)
    def _(step):
        w = wide_of(step)
        for copy in load(w):
            copy.wait()
        local_wide(w)
        core_copy(lax.rem(w, 2), w // 2).start()

        @pl.when((step >= 1) & (step <= CHUNKS))
        def _():
            core_copy(1 - row, step - 1).wait_recv()
            for part in range(2):
                pair_join(1 - row, 2 * step - 2 + part)
                row_copy(2 * step - 2 + part).start()

    one_parts[...] = three_lanes(jnp.exp2(-jnp.abs(cum - cum[2 * SUB - 1 : 2 * SUB])))
    two_parts[...] = three_lanes(jnp.exp2(-jnp.abs(cum - jnp.concatenate(
        [jnp.broadcast_to(cum[at : at + 1], (2 * SUB, 128)) for at in (SUB - 1, 3 * SUB - 1)],
        axis=0))))
    scores = contract(b_ref[...], c_ref[...], 1, 1)
    cross_ref[...] = scores.astype(BF16)
    turned_ref[...] = contract(c_ref[...], b_ref[...], 1, 1).astype(BF16)
    upper = lax.broadcasted_iota(jnp.int32, (SUB, SUB), 0) <= lax.broadcasted_iota(
        jnp.int32, (SUB, SUB), 1)
    for sub in range(4):
        rows = slice(sub * SUB, (sub + 1) * SUB)
        diag_ref[sub] = jnp.where(upper, scores[rows, rows], 0.0)
    pairs_ref[...] = jnp.zeros_like(pairs_ref)
    ends_ref[...] = jnp.zeros_like(ends_ref)
    read_sum[...] = jnp.zeros_like(read_sum)
    write_sum[...] = jnp.zeros_like(write_sum)

    def block_wide(w):
        columns = columns_of(w)
        spread = jnp.where(heads_ref[...] == 4 * w, 1.0, 0.0).astype(BF16)
        one = contract(one_parts[...], spread, 1, 0)
        two = contract(two_parts[...], spread, 1, 0)
        x, g = x_ref[:, columns], g_ref[:, columns]
        half = 2 * SUB
        x_one = (x[:half].astype(F32) * one[:half]).astype(BF16)
        g_one = (g[half:].astype(F32) * one[half:]).astype(BF16)
        pairs_ref[:half, half:] += contract(x_one, g_one, 1, 1)
        back_one = contract(cross_ref[:half, half:], g_one, 1, 0)
        out_one = contract(turned_ref[half:, :half], x_one, 1, 0)
        flow_one = [x_one.astype(F32) * back_one, g_one.astype(F32) * out_one]
        lanes = lax.broadcasted_iota(jnp.int32, (SUB, 128), 1)
        zero = jnp.zeros((), BF16)
        out_dots = [[] for _ in range(4)]
        cum_heads = [cumrow_ref[pl.ds(4 * w + h, 1), :] for h in range(4)]
        for side in range(2):
            early = slice(side * half, side * half + SUB)
            late = slice(side * half + SUB, (side + 1) * half)
            x_two = (x[early].astype(F32) * two[early]).astype(BF16)
            g_two = (g[late].astype(F32) * two[late]).astype(BF16)
            pairs_ref[early, late] += contract(x_two, g_two, 1, 1)
            back_two = contract(cross_ref[early, late], g_two, 1, 0)
            out_two = contract(turned_ref[late, early], x_two, 1, 0)
            flow_two = [-(x_two.astype(F32) * back_two), g_two.astype(F32) * out_two]
            for part, rows in enumerate((early, late)):
                local = slice(part * SUB, (part + 1) * SUB)
                if side == 0:
                    flow = flow_two[part] - flow_one[0][local]
                    within = one[rows] * back_one[local]
                    if part == 0:
                        within = within + two[rows] * back_two
                else:
                    flow = flow_two[part] + flow_one[1][local]
                    within = two[rows] * back_two if part == 0 else None
                sub = 2 * side + part
                scores = diag_ref[sub]
                scores = jnp.concatenate([scores, scores], axis=1)
                added = pairs_ref[rows, rows]
                for pair in range(2):
                    place = slice(pair * 128, (pair + 1) * 128)
                    xs, gs = x[rows, place], g[rows, place]
                    g_split = jnp.concatenate(
                        [jnp.where(lanes < P_SIZE, gs, zero), jnp.where(lanes >= P_SIZE, gs, zero)],
                        axis=0)
                    products = contract(xs, g_split, 1, 1)
                    gap = jnp.concatenate(
                        [lane_pick(cum_ref[rows, :], 4 * w + 2 * pair + h) for h in range(2)],
                        axis=1)
                    cum_rows = jnp.concatenate(
                        [cum_heads[2 * pair + h][:, rows] for h in range(2)],
                        axis=1)
                    decay = jnp.exp2(jnp.minimum(cum_rows - gap, 0.0))
                    decayed = products * decay
                    added = added + decayed[:, :SUB] + decayed[:, SUB:]
                    mixing = (scores * decay).astype(BF16)
                    out_dot = jnp.sum(mixing.astype(F32) * products, axis=0, keepdims=True)
                    for h in range(2):
                        out_dots[2 * pair + h].append(out_dot[:, h * SUB : (h + 1) * SUB])
                    back = contract(mixing, g_split, 1, 0)
                    at = pl.ds(pl.multiple_of(w * WIDE + pair * 128, 128), 128)
                    within_ref[rows, at] = back if within is None else within[:, place] + back
                    flow_ref[rows, at] = flow[:, place] - xs.astype(F32) * back
                pairs_ref[rows, rows] = added
        for h in range(4):
            outdot_ref[pl.ds(4 * w + h, 1), :] = jnp.concatenate(out_dots[h], axis=1)

    def send_enter(m, enter):
        enter_out[m] = group_buf[m, 2 * HALF : 2 * HALF + 1] * enter + group_buf[m, :HALF]
        enter_copy(m).start()

    def send_leave(m, leave):
        leave_out[m] = group_buf[m, 2 * HALF : 2 * HALF + 1] * leave + group_buf[m, HALF : 2 * HALF]
        leave_copy(m).start()

    def take_enter(m):
        @pl.when(is_first)
        def _():
            enter_in[m] = jnp.zeros((HALF, CHUNK), F32)

        @pl.when(jnp.logical_not(is_first))
        def _():
            enter_copy(m).wait_recv()

        @pl.when(jnp.logical_not(is_last))
        def _():
            send_enter(m, enter_in[m])

    def take_leave(m):
        @pl.when(is_last)
        def _():
            leave_in[m] = jnp.zeros((HALF, CHUNK), F32)

        @pl.when(jnp.logical_not(is_last))
        def _():
            leave_copy(m).wait_recv()

        @pl.when(jnp.logical_not(is_first))
        def _():
            send_leave(m, leave_in[m])

    def carried(w, side):
        rows = slice(side * HALF, (side + 1) * HALF)
        return jnp.concatenate([
            jnp.concatenate([carry_ref[4 * w + 2 * q + part, rows] for part in range(2)], axis=0)
            for q in range(2)], axis=1)

    def final_wide(w):
        columns = columns_of(w)
        enter, leave = carried(w, 0), carried(w, 1)
        enter_two, leave_two = split_two(enter), split_two(leave)
        b, c = b_ref[...], c_ref[...]
        gw, xw = gw_ref[:, columns], xw_ref[:, columns]
        out = contract(jnp.concatenate([c, c], axis=1), jnp.concatenate(enter_two, axis=0), 1, 0)
        back = contract(jnp.concatenate([b, b], axis=1), jnp.concatenate(leave_two, axis=0), 1, 0)
        grad_ref[:, columns] = (
            within_ref[:, columns] + back * tail_ref[:, columns]
        ).astype(BF16)
        read_sum[...] += sum(contract(gw, part, 1, 1) for part in enter_two)
        write_sum[...] += sum(contract(xw, part, 1, 1) for part in leave_two)
        flow = flow_ref[:, columns] + gw.astype(F32) * out - xw.astype(F32) * back
        place = lax.broadcasted_iota(jnp.int32, (16, WIDE), 0)
        lanes = lax.broadcasted_iota(jnp.int32, (16, WIDE), 1)
        pick = jnp.where(lanes // P_SIZE == place, 1.0, 0.0).astype(BF16)
        sums = sum(contract(pick, part, 1, 1) for part in split_two(flow))
        for h in range(4):
            flowrow_ref[pl.ds(4 * w + h, 1), :] = sums[h : h + 1]
        for q in range(2):
            lanes = slice(q * CHUNK, (q + 1) * CHUNK)
            mine = 4 * w + 2 * q
            local = jnp.concatenate([pay_ref[mine + part, :HALF] for part in range(2)], axis=0)
            state = pay_ref[mine, 2 * HALF : 2 * HALF + 1] * enter[:, lanes] + local
            ends_ref[pl.ds(2 * w + q, 1), :] = jnp.sum(
                state * leave[:, lanes], axis=0, keepdims=True)

    def final_level(r, m, enter, leave):
        slot = r * PARTS + m
        mine = part_of(r, m, core)
        own, far = descend(is_core_late, pay_ref[mine], core_in[slot], enter, leave)
        back_out[slot, :HALF], back_out[slot, HALF:] = far
        back_copy(r, m).start()
        carry_ref[mine, :HALF], carry_ref[mine, HALF:] = own

    def group_join(m):
        @pl.when(lax.rem(m, 2) == 0)
        def _():
            core_copy(row, m // 2).wait_recv()
            for r in range(2):
                core_copy(r, m // 2).wait_send()

        pair_join(row, m)
        row_copy(m).wait_recv()
        early, late = ordered(is_row_late, pair_buf[row * PARTS + m], row_in[m])
        join(early, late, group_buf, m)

    def finish(m):
        own, far = descend(is_row_late, pair_buf[row * PARTS + m], row_in[m], enter_in[m],
                           leave_in[m])
        down_out[m, :HALF], down_out[m, HALF:] = far
        down_copy(m).start()
        final_level(row, m, *own)
        row_copy(m).wait_send()

    def down(m):
        down_copy(m).wait_recv()
        final_level(1 - row, m, down_in[m, :HALF], down_in[m, HALF:])

    def take_back(r, m):
        back_copy(r, m).wait_recv()
        carry_ref[part_of(r, m, 1 - core)] = back_in[r * PARTS + m]

        @pl.when(lax.rem(m, 2) == 1)
        def _():
            final_wide(m - 1 + r)

        back_copy(r, m).wait_send()

    def take_near(m):
        take_back(row, m)

        @pl.when(jnp.logical_not(is_last))
        def _():
            enter_copy(m).wait_send()

        @pl.when(jnp.logical_not(is_first))
        def _():
            leave_copy(m).wait_send()

    def take_far(m):
        take_back(1 - row, m)
        down_copy(m).wait_send()

    def stage(j, start, act):
        m = (j - start) // SPACING
        due = (j >= start) & (j < start + SPACING * PARTS) & (lax.rem(j - start, SPACING) == 0)

        @pl.when(due)
        def _():
            act(m)

    enter_start = JOIN_START + HOP * rank
    leave_start = JOIN_START + HOP * (ranks - 1 - rank)
    finish_start = jnp.maximum(enter_start, leave_start)
    down_start = finish_start + DOWN_LAG
    slots = JOIN_START + HOP * (ranks - 1) + DOWN_LAG + NEAR_LAG + SPACING * PARTS

    @pl.loop(0, slots)
    def _(j):
        stage(j, JOIN_START, group_join)
        stage(j, enter_start, take_enter)
        stage(j, leave_start, take_leave)
        stage(j, finish_start, finish)
        stage(j, finish_start + NEAR_LAG, take_near)
        stage(j, down_start, down)
        stage(j, down_start + NEAR_LAG, take_far)

        @pl.when(j < WIDES)
        def _():
            block_wide(2 * lax.rem(j, CHUNKS) + j // CHUNKS)

        @pl.when(j == WIDES)
        def _():
            first = lax.broadcasted_iota(jnp.int32, (BLOCK, BLOCK), 0)
            second = lax.broadcasted_iota(jnp.int32, (BLOCK, BLOCK), 1)
            pairs = jnp.where(first <= second, pairs_ref[...], 0.0).astype(BF16)
            read_sum[...] += contract(pairs, b_ref[...], 0, 0)
            write_sum[...] += contract(pairs, c_ref[...], 1, 0)

    read_ref[...] = read_sum[...].astype(BF16)
    write_ref[...] = write_sum[...].astype(BF16)
    heads = lax.broadcasted_iota(jnp.int32, (HEADS, 32), 0)
    chunks = lax.broadcasted_iota(jnp.int32, (HEADS, 32), 1)
    pick = jnp.where(heads // 2 == chunks, 1.0, 0.0).astype(BF16)
    ends = sum(contract(pick, part, 1, 0) for part in split_three(ends_ref[...]))
    heads = lax.broadcasted_iota(jnp.int32, (HEADS, 128), 0)
    entries = lax.broadcasted_iota(jnp.int32, (HEADS, 128), 1)
    own_head = entries // P_SIZE == lax.rem(heads, 2)
    total = jnp.sum(jnp.where(own_head, ends, 0.0), axis=1, keepdims=True)
    flows = flowrow_ref[...] + outdot_ref[...]
    decay_ref[...] = total + three_sums(flows, lower_ref[...], 0)


def whole_call(x, g, b, c, rates, ranks):
    half, one = 2 * PARTS, PARTS

    def buffer(count, rows):
        return pltpu.VMEM((count, rows, CHUNK), F32)

    def wide(dtype):
        return pltpu.VMEM((BLOCK, WIDTH), dtype)

    def square(dtype):
        return pltpu.VMEM((BLOCK, BLOCK), dtype)

    def parts():
        return pltpu.VMEM((BLOCK, 128), BF16)

    def rows():
        return pltpu.VMEM((HEADS, BLOCK), F32)

    counts = [one, one] + [one] * 8 + [half, half]
    return pl.pallas_call(
        functools.partial(whole_kernel, ranks),
        out_shape=[
            pltpu.VMEM((BLOCK, WIDTH), BF16),
            pltpu.VMEM((BLOCK, N), BF16),
            pltpu.VMEM((BLOCK, N), BF16),
            pltpu.VMEM((HEADS, BLOCK), F32),
        ],
        in_specs=[pl.BlockSpec(memory_space=pltpu.HBM)] * 5,
        out_specs=[pl.BlockSpec(memory_space=pltpu.VMEM)] * 4,
        scratch_shapes=[
            wide(BF16), wide(BF16), parts(), parts(), rows(),
            wide(BF16), wide(BF16), wide(F32), wide(F32), wide(F32),
            rows(), rows(), rows(), pltpu.VMEM((32, CHUNK), F32),
            pltpu.VMEM((BLOCK, N), F32), pltpu.VMEM((BLOCK, N), F32),
            parts(), parts(), parts(), parts(), pltpu.VMEM((BLOCK, 128), F32),
            pltpu.VMEM((128, WIDE), jnp.int32),
            pltpu.VMEM((N, BLOCK), BF16), pltpu.VMEM((N, BLOCK), BF16),
            buffer(2 * half, PAY), buffer(2 * half, 2 * HALF),
            square(BF16), square(BF16), square(BF16), pltpu.VMEM((4, SUB, SUB), F32), square(F32),
            buffer(half, PAY), buffer(half, PAY), buffer(one, PAY), buffer(one, PAY),
            buffer(one, HALF), buffer(one, HALF), buffer(one, HALF), buffer(one, HALF),
            buffer(one, 2 * HALF), buffer(one, 2 * HALF), buffer(half, 2 * HALF),
            buffer(half, 2 * HALF),
            pltpu.SemaphoreType.DMA((WIDES,)), pltpu.SemaphoreType.DMA((WIDES,)),
            pltpu.SemaphoreType.DMA((3,)),
        ] + [pltpu.SemaphoreType.DMA((count,)) for count in counts],
        compiler_params=pltpu.CompilerParams(
            vmem_limit_bytes=VMEM_BYTES, collective_id=0, has_side_effects=True
        ),
    )(x, g, b, c, rates)


def store_kernel(*refs):
    sources, targets, sems = refs[:4], refs[4:8], refs[8]
    copies = [
        pltpu.make_async_copy(source, target, sems.at[index])
        for index, (source, target) in enumerate(zip(sources, targets))
    ]
    for copy in copies:
        copy.start()
    for copy in copies:
        copy.wait()


def store_call(results):
    return pl.pallas_call(
        store_kernel,
        out_shape=[jax.ShapeDtypeStruct(result.shape, result.dtype) for result in results],
        in_specs=[pl.BlockSpec(memory_space=pl.ANY)] * 4,
        out_specs=[pl.BlockSpec(memory_space=pl.ANY)] * 4,
        scratch_shapes=[pltpu.SemaphoreType.DMA((4,))],
        compiler_params=pltpu.CompilerParams(vmem_limit_bytes=COPY_BYTES),
    )(*results)


def body(inputs, write_vectors, read_vectors, log_decay, grad_out, *, seq_size):
    results = whole_call(
        inputs, grad_out, write_vectors, read_vectors, log_decay, seq_size // 4
    )
    return tuple(store_call(results))


def solution(mesh):
    rows = P(("grp", "seq"), None)
    columns = P(None, ("grp", "seq"))
    return jax.shard_map(
        functools.partial(body, seq_size=mesh.shape["seq"]),
        mesh=mesh,
        in_specs=(rows, rows, rows, columns, rows),
        out_specs=(rows, rows, rows, columns),
        check_vma=False,
    )
```

```python
import functools
import jax
import jax.numpy as jnp
from jax import lax
from jax.experimental import pallas as pl
from jax.experimental.pallas import tpu as pltpu
from jax.sharding import PartitionSpec as P

HEADS = 40
P_SIZE = 64
N = 128
BLOCK = 512
WIDTH = HEADS * P_SIZE
CHUNK = 128
WIDE = 256
CHUNKS = WIDTH // (4 * CHUNK)
WIDES = WIDTH // WIDE
SUB = 128
HALF = N // 2
PARTS = 2 * CHUNKS
PAY = 2 * HALF + 8
SENT = 2 * HALF + 1
LOG2E = 1.4426950408889634
F32 = jnp.float32
BF16 = jnp.bfloat16
VMEM_BYTES = 53 * 1024 * 1024
COPY_BYTES = 1024 * 1024


def split_two(values):
    upper = values.astype(BF16)
    return upper, (values - upper.astype(F32)).astype(BF16)


def split_three(values):
    upper = values.astype(BF16)
    rest = values - upper.astype(F32)
    middle = rest.astype(BF16)
    return upper, middle, (rest - middle.astype(F32)).astype(BF16)


def contract(left, right, left_dim, right_dim):
    return lax.dot_general(
        left, right, (((left_dim,), (right_dim,)), ((), ())), preferred_element_type=F32
    )


def lower_ones():
    rows = lax.broadcasted_iota(jnp.int32, (BLOCK, BLOCK), 0)
    columns = lax.broadcasted_iota(jnp.int32, (BLOCK, BLOCK), 1)
    return jnp.where(rows >= columns, 1.0, 0.0).astype(BF16)


def parts_of(pay):
    return pay[:HALF], pay[HALF : 2 * HALF], pay[2 * HALF : 2 * HALF + 1]


def join(early, late, out_ref, index):
    early_s, early_r, early_d = parts_of(early)
    late_s, late_r, late_d = parts_of(late)
    out_ref[index, :HALF] = late_d * early_s + late_s
    out_ref[index, HALF : 2 * HALF] = early_r + early_d * late_r
    out_ref[index, 2 * HALF :] = jnp.broadcast_to(early_d * late_d, (8, CHUNK))


def ordered(is_late, mine, other):
    return jnp.where(is_late, other, mine), jnp.where(is_late, mine, other)


def descend(is_late, mine, other, enter, leave):
    early, late = ordered(is_late, mine, other)
    early_s, _, early_d = parts_of(early)
    _, late_r, late_d = parts_of(late)
    first_leave = late_r + late_d * leave
    second_enter = early_d * enter + early_s
    own = (jnp.where(is_late, second_enter, enter), jnp.where(is_late, leave, first_leave))
    far = (jnp.where(is_late, enter, second_enter), jnp.where(is_late, first_leave, leave))
    return own, far


JOIN_START = 0
SPACING = 1
HOP = 3
DOWN_LAG = 4
NEAR_LAG = 1
EARLY = 7


def three_lanes(values):
    lanes = lax.broadcasted_iota(jnp.int32, values.shape, 1)
    upper, middle, rest = [part.astype(F32) for part in split_three(values)]
    picked = jnp.where(lanes < HEADS, upper, jnp.where(lanes < 2 * HEADS, middle, rest))
    return jnp.where(lanes < 3 * HEADS, picked, 0.0).astype(BF16)


def three_sums(values, square, square_dim):
    stacked = jnp.concatenate(
        [part.astype(F32) for part in split_three(values)] + [jnp.zeros((8, BLOCK), F32)], axis=0
    ).astype(BF16)
    sums = contract(stacked, square, 1, square_dim)
    return sums[:HEADS] + sums[HEADS : 2 * HEADS] + sums[2 * HEADS : 3 * HEADS]


def lane_pick(values, lane):
    index = jnp.full(values.shape, lane, jnp.int32)
    return jnp.take_along_axis(values, index, axis=1, mode="promise_in_bounds")


def whole_kernel(ranks, x_hbm, g_hbm, b_hbm, c_hbm, rate_hbm,
                 grad_ref, write_ref, read_ref, decay_ref,
                 x_ref, g_ref, b_ref, c_ref, rate_ref,
                 xw_ref, gw_ref, tail_ref, within_ref, flow_ref,
                 cumrow_ref, outdot_ref, flowrow_ref, ends_ref,
                 read_sum, write_sum, growth_parts, tail_parts, one_parts, two_parts, cum_ref,
                 heads_ref, b_turned, c_turned, pay_ref, carry_ref,
                 lower_ref, cross_ref, turned_ref, diag_ref, pairs_ref, core_in, pair_buf, row_in, group_buf,
                 enter_in, enter_out, leave_in, leave_out, down_out, down_in, back_out, back_in,
                 x_sem, g_sem, small_sem,
                 core_send, core_recv, row_send, row_recv, enter_send, enter_recv, leave_send,
                 leave_recv, down_send, down_recv, back_send, back_recv):
    me = lax.axis_index("seq")
    core = lax.rem(me, 2)
    row = lax.rem(me // 2, 2)
    rank = me // 4
    core_peer = me + 1 - 2 * core
    row_peer = me + 2 - 4 * row
    is_first, is_last = rank == 0, rank == ranks - 1

    def remote(source, target, send, recv, peer):
        return pltpu.make_async_remote_copy(
            src_ref=source, dst_ref=target, send_sem=send, recv_sem=recv,
            device_id={"seq": peer}, device_id_type=pl.DeviceIdType.MESH,
        )

    def chunk_of(r, k, q):
        return 4 * k + 2 * r + q

    def core_copy(r, k):
        slot = r * CHUNKS + k
        mine = pay_ref.at[pl.ds(2 * chunk_of(r, k, 1 - core), 2)]
        return remote(mine, core_in.at[pl.ds(2 * slot, 2)], core_send.at[slot],
                      core_recv.at[slot], core_peer)

    def row_copy(m):
        sent = pl.ds(0, SENT)
        return remote(pair_buf.at[(1 - row) * PARTS + m, sent], row_in.at[m, sent],
                      row_send.at[m], row_recv.at[m], row_peer)

    def enter_copy(m):
        return remote(enter_out.at[m], enter_in.at[m], enter_send.at[m], enter_recv.at[m], me + 4)

    def leave_copy(m):
        return remote(leave_out.at[m], leave_in.at[m], leave_send.at[m], leave_recv.at[m], me - 4)

    def down_copy(m):
        return remote(down_out.at[m], down_in.at[m], down_send.at[m], down_recv.at[m], row_peer)

    def back_copy(r, m):
        slot = r * PARTS + m
        return remote(back_out.at[slot], back_in.at[slot], back_send.at[slot], back_recv.at[slot],
                      core_peer)

    def part_of(r, m, q):
        return 2 * chunk_of(r, m // 2, q) + lax.rem(m, 2)

    def wide_of(step):
        return 2 * lax.rem(step, CHUNKS) + jnp.where(step < CHUNKS, 1 - row, row)

    def columns_of(w):
        return pl.ds(pl.multiple_of(w * WIDE, WIDE), WIDE)

    def load(w):
        return (pltpu.make_async_copy(x_hbm.at[:, columns_of(w)], x_ref.at[:, columns_of(w)],
                                      x_sem.at[w]),
                pltpu.make_async_copy(g_hbm.at[:, columns_of(w)], g_ref.at[:, columns_of(w)],
                                      g_sem.at[w]))

    small = [pltpu.make_async_copy(source, target, small_sem.at[index])
             for index, (source, target) in enumerate(
                 ((rate_hbm, rate_ref), (b_hbm, b_ref), (c_hbm, c_ref)))]
    for copy in small:
        copy.start()

    @pl.loop(0, WIDES)
    def _(step):
        for copy in load(wide_of(step)):
            copy.start()

    barrier = pltpu.get_barrier_semaphore()

    def greet(peer):
        pl.semaphore_signal(barrier, inc=1, device_id={"seq": peer},
                            device_id_type=pl.DeviceIdType.MESH)

    greet(core_peer)
    greet(row_peer)

    @pl.when(jnp.logical_not(is_first))
    def _():
        greet(me - 4)

    @pl.when(jnp.logical_not(is_last))
    def _():
        greet(me + 4)

    source = lax.broadcasted_iota(jnp.int32, (128, WIDE), 0)
    target = lax.broadcasted_iota(jnp.int32, (128, WIDE), 1)
    head = source - jnp.where(source >= HEADS, HEADS, 0) - jnp.where(source >= 2 * HEADS, HEADS, 0)
    head = jnp.where(source < 3 * HEADS, head, 4 * HEADS)
    heads_ref[...] = head - target // P_SIZE

    lower_ref[...] = lower_ones()
    small[0].wait()
    cum_rows = three_sums(rate_ref[...] * LOG2E, lower_ref[...], 1)
    cumrow_ref[...] = cum_rows
    cum = jnp.concatenate([cum_rows, cum_rows, cum_rows, jnp.zeros((8, BLOCK), F32)], axis=0).T
    growth_parts[...] = three_lanes(jnp.exp2(cum))
    tail_parts[...] = three_lanes(jnp.exp2(cum[BLOCK - 1 :] - cum))
    for copy in small[1:]:
        copy.wait()
    b_turned[...] = b_ref[...].astype(F32).T.astype(BF16)
    c_turned[...] = c_ref[...].astype(F32).T.astype(BF16)
    cum_ref[...] = cum

    def local_wide(w):
        columns = columns_of(w)
        spread = jnp.where(heads_ref[...] == 4 * w, 1.0, 0.0).astype(BF16)
        growth = contract(growth_parts[...], spread, 1, 0)
        tail = contract(tail_parts[...], spread, 1, 0)
        x_weighted = (x_ref[:, columns].astype(F32) * tail).astype(BF16)
        g_weighted = (g_ref[:, columns].astype(F32) * growth).astype(BF16)
        xw_ref[:, columns] = x_weighted
        gw_ref[:, columns] = g_weighted
        tail_ref[:, columns] = tail
        state = contract(b_turned[...], x_weighted, 1, 0)
        adjoint = contract(c_turned[...], g_weighted, 1, 0)
        decay = jnp.broadcast_to(growth[BLOCK - 1 :], (8, WIDE))
        for q in range(2):
            lanes = slice(q * CHUNK, (q + 1) * CHUNK)
            for part in range(2):
                rows = slice(part * HALF, (part + 1) * HALF)
                mine = 2 * (2 * w + q) + part
                pay_ref[mine, :HALF] = state[rows, lanes]
                pay_ref[mine, HALF : 2 * HALF] = adjoint[rows, lanes]
                pay_ref[mine, 2 * HALF :] = decay[:, lanes]

    is_core_late, is_row_late = core == 1, row == 1

    def pair_join(r, m):
        slot = r * PARTS + m
        early, late = ordered(is_core_late, pay_ref[part_of(r, m, core)], core_in[slot])
        join(early, late, pair_buf, slot)

    chain_peers = jnp.where(is_first, 0, 1) + jnp.where(is_last, 0, 1)
    pl.semaphore_wait(barrier, 2 + chain_peers)

    def local_step(step):
        w = wide_of(step)
        for copy in load(w):
            copy.wait()
        local_wide(w)
        core_copy(lax.rem(w, 2), w // 2).start()

    @pl.loop(0, EARLY)
    def _(step):
        local_step(step)

        @pl.when((step >= 1) & (step <= CHUNKS))
        def _():
            core_copy(1 - row, step - 1).wait_recv()
            for part in range(2):
                pair_join(1 - row, 2 * step - 2 + part)
                row_copy(2 * step - 2 + part).start()

    pairs_ref[...] = jnp.zeros_like(pairs_ref)
    ends_ref[...] = jnp.zeros_like(ends_ref)
    read_sum[...] = jnp.zeros_like(read_sum)
    write_sum[...] = jnp.zeros_like(write_sum)

    def prepare_block():
        one_parts[...] = three_lanes(jnp.exp2(-jnp.abs(cum_ref[...] - cum_ref[2 * SUB - 1 : 2 * SUB])))
        two_parts[...] = three_lanes(jnp.exp2(-jnp.abs(cum_ref[...] - jnp.concatenate(
            [jnp.broadcast_to(cum_ref[at : at + 1], (2 * SUB, 128)) for at in (SUB - 1, 3 * SUB - 1)],
            axis=0))))
        scores = contract(b_ref[...], c_ref[...], 1, 1)
        cross_ref[...] = scores.astype(BF16)
        turned_ref[...] = contract(c_ref[...], b_ref[...], 1, 1).astype(BF16)
        upper = lax.broadcasted_iota(jnp.int32, (SUB, SUB), 0) <= lax.broadcasted_iota(
            jnp.int32, (SUB, SUB), 1)
        for sub in range(4):
            rows = slice(sub * SUB, (sub + 1) * SUB)
            diag_ref[sub] = jnp.where(upper, scores[rows, rows], 0.0)

    def block_wide(w):
        columns = columns_of(w)
        spread = jnp.where(heads_ref[...] == 4 * w, 1.0, 0.0).astype(BF16)
        one = contract(one_parts[...], spread, 1, 0)
        two = contract(two_parts[...], spread, 1, 0)
        x, g = x_ref[:, columns], g_ref[:, columns]
        half = 2 * SUB
        x_one = (x[:half].astype(F32) * one[:half]).astype(BF16)
        g_one = (g[half:].astype(F32) * one[half:]).astype(BF16)
        pairs_ref[:half, half:] += contract(x_one, g_one, 1, 1)
        back_one = contract(cross_ref[:half, half:], g_one, 1, 0)
        out_one = contract(turned_ref[half:, :half], x_one, 1, 0)
        flow_one = [x_one.astype(F32) * back_one, g_one.astype(F32) * out_one]
        lanes = lax.broadcasted_iota(jnp.int32, (SUB, 128), 1)
        zero = jnp.zeros((), BF16)
        out_dots = [[] for _ in range(4)]
        cum_heads = [cumrow_ref[pl.ds(4 * w + h, 1), :] for h in range(4)]
        for side in range(2):
            early = slice(side * half, side * half + SUB)
            late = slice(side * half + SUB, (side + 1) * half)
            x_two = (x[early].astype(F32) * two[early]).astype(BF16)
            g_two = (g[late].astype(F32) * two[late]).astype(BF16)
            pairs_ref[early, late] += contract(x_two, g_two, 1, 1)
            back_two = contract(cross_ref[early, late], g_two, 1, 0)
            out_two = contract(turned_ref[late, early], x_two, 1, 0)
            flow_two = [-(x_two.astype(F32) * back_two), g_two.astype(F32) * out_two]
            for part, rows in enumerate((early, late)):
                local = slice(part * SUB, (part + 1) * SUB)
                if side == 0:
                    flow = flow_two[part] - flow_one[0][local]
                    within = one[rows] * back_one[local]
                    if part == 0:
                        within = within + two[rows] * back_two
                else:
                    flow = flow_two[part] + flow_one[1][local]
                    within = two[rows] * back_two if part == 0 else None
                sub = 2 * side + part
                scores = diag_ref[sub]
                scores = jnp.concatenate([scores, scores], axis=1)
                added = pairs_ref[rows, rows]
                for pair in range(2):
                    place = slice(pair * 128, (pair + 1) * 128)
                    xs, gs = x[rows, place], g[rows, place]
                    g_split = jnp.concatenate(
                        [jnp.where(lanes < P_SIZE, gs, zero), jnp.where(lanes >= P_SIZE, gs, zero)],
                        axis=0)
                    products = contract(xs, g_split, 1, 1)
                    gap = jnp.concatenate(
                        [lane_pick(cum_ref[rows, :], 4 * w + 2 * pair + h) for h in range(2)],
                        axis=1)
                    cum_rows = jnp.concatenate(
                        [cum_heads[2 * pair + h][:, rows] for h in range(2)],
                        axis=1)
                    decay = jnp.exp2(jnp.minimum(cum_rows - gap, 0.0))
                    decayed = products * decay
                    added = added + decayed[:, :SUB] + decayed[:, SUB:]
                    mixing = (scores * decay).astype(BF16)
                    out_dot = jnp.sum(mixing.astype(F32) * products, axis=0, keepdims=True)
                    for h in range(2):
                        out_dots[2 * pair + h].append(out_dot[:, h * SUB : (h + 1) * SUB])
                    back = contract(mixing, g_split, 1, 0)
                    at = pl.ds(pl.multiple_of(w * WIDE + pair * 128, 128), 128)
                    within_ref[rows, at] = back if within is None else within[:, place] + back
                    flow_ref[rows, at] = flow[:, place] - xs.astype(F32) * back
                pairs_ref[rows, rows] = added
        for h in range(4):
            outdot_ref[pl.ds(4 * w + h, 1), :] = jnp.concatenate(out_dots[h], axis=1)

    def send_enter(m, enter):
        enter_out[m] = group_buf[m, 2 * HALF : 2 * HALF + 1] * enter + group_buf[m, :HALF]
        enter_copy(m).start()

    def send_leave(m, leave):
        leave_out[m] = group_buf[m, 2 * HALF : 2 * HALF + 1] * leave + group_buf[m, HALF : 2 * HALF]
        leave_copy(m).start()

    def take_enter(m):
        @pl.when(is_first)
        def _():
            enter_in[m] = jnp.zeros((HALF, CHUNK), F32)

        @pl.when(jnp.logical_not(is_first))
        def _():
            enter_copy(m).wait_recv()

        @pl.when(jnp.logical_not(is_last))
        def _():
            send_enter(m, enter_in[m])

    def take_leave(m):
        @pl.when(is_last)
        def _():
            leave_in[m] = jnp.zeros((HALF, CHUNK), F32)

        @pl.when(jnp.logical_not(is_last))
        def _():
            leave_copy(m).wait_recv()

        @pl.when(jnp.logical_not(is_first))
        def _():
            send_leave(m, leave_in[m])

    def carried(w, side):
        rows = slice(side * HALF, (side + 1) * HALF)
        return jnp.concatenate([
            jnp.concatenate([carry_ref[4 * w + 2 * q + part, rows] for part in range(2)], axis=0)
            for q in range(2)], axis=1)

    def final_wide(w):
        columns = columns_of(w)
        enter, leave = carried(w, 0), carried(w, 1)
        enter_two, leave_two = split_two(enter), split_two(leave)
        b, c = b_ref[...], c_ref[...]
        gw, xw = gw_ref[:, columns], xw_ref[:, columns]
        out = contract(jnp.concatenate([c, c], axis=1), jnp.concatenate(enter_two, axis=0), 1, 0)
        back = contract(jnp.concatenate([b, b], axis=1), jnp.concatenate(leave_two, axis=0), 1, 0)
        grad_ref[:, columns] = (
            within_ref[:, columns] + back * tail_ref[:, columns]
        ).astype(BF16)
        read_sum[...] += sum(contract(gw, part, 1, 1) for part in enter_two)
        write_sum[...] += sum(contract(xw, part, 1, 1) for part in leave_two)
        flow = flow_ref[:, columns] + gw.astype(F32) * out - xw.astype(F32) * back
        place = lax.broadcasted_iota(jnp.int32, (16, WIDE), 0)
        lanes = lax.broadcasted_iota(jnp.int32, (16, WIDE), 1)
        pick = jnp.where(lanes // P_SIZE == place, 1.0, 0.0).astype(BF16)
        sums = sum(contract(pick, part, 1, 1) for part in split_two(flow))
        for h in range(4):
            flowrow_ref[pl.ds(4 * w + h, 1), :] = sums[h : h + 1]
        for q in range(2):
            lanes = slice(q * CHUNK, (q + 1) * CHUNK)
            mine = 4 * w + 2 * q
            local = jnp.concatenate([pay_ref[mine + part, :HALF] for part in range(2)], axis=0)
            state = pay_ref[mine, 2 * HALF : 2 * HALF + 1] * enter[:, lanes] + local
            ends_ref[pl.ds(2 * w + q, 1), :] = jnp.sum(
                state * leave[:, lanes], axis=0, keepdims=True)

    def final_chunk(chunk):
        columns = pl.ds(pl.multiple_of(chunk * CHUNK, CHUNK), CHUNK)
        enter = jnp.concatenate([carry_ref[2 * chunk + part, :HALF] for part in range(2)], axis=0)
        leave = jnp.concatenate([carry_ref[2 * chunk + part, HALF:] for part in range(2)], axis=0)
        enter_high, enter_low = split_two(enter)
        leave_high, leave_low = split_two(leave)
        b, c = b_ref[...], c_ref[...]
        gw, xw = gw_ref[:, columns], xw_ref[:, columns]
        out = contract(jnp.concatenate([c, c], axis=1),
                       jnp.concatenate([enter_high, enter_low], axis=0), 1, 0)
        back = contract(jnp.concatenate([b, b], axis=1),
                        jnp.concatenate([leave_high, leave_low], axis=0), 1, 0)
        grad_ref[:, columns] = (
            within_ref[:, columns] + back * tail_ref[:, columns]
        ).astype(BF16)
        read_sum[...] += contract(jnp.concatenate([gw, gw], axis=1),
                                  jnp.concatenate([enter_high, enter_low], axis=1), 1, 1)
        write_sum[...] += contract(jnp.concatenate([xw, xw], axis=1),
                                   jnp.concatenate([leave_high, leave_low], axis=1), 1, 1)
        flow = flow_ref[:, columns] + gw.astype(F32) * out - xw.astype(F32) * back
        place = lax.broadcasted_iota(jnp.int32, (16, 256), 0)
        lanes = lax.broadcasted_iota(jnp.int32, (16, 256), 1)
        pick = jnp.where(lax.rem(lanes // P_SIZE, 2) == place, 1.0, 0.0).astype(BF16)
        sums = contract(pick, jnp.concatenate(split_two(flow), axis=1), 1, 1)
        for h in range(2):
            flowrow_ref[pl.ds(2 * chunk + h, 1), :] = sums[h : h + 1]
        local = jnp.concatenate([pay_ref[2 * chunk + part, :HALF] for part in range(2)], axis=0)
        end_state = pay_ref[2 * chunk, 2 * HALF : 2 * HALF + 1] * enter + local
        ends_ref[pl.ds(chunk, 1), :] = jnp.sum(end_state * leave, axis=0, keepdims=True)

    def final_level(r, m, enter, leave):
        slot = r * PARTS + m
        mine = part_of(r, m, core)
        own, far = descend(is_core_late, pay_ref[mine], core_in[slot], enter, leave)
        back_out[slot, :HALF], back_out[slot, HALF:] = far
        back_copy(r, m).start()
        carry_ref[mine, :HALF], carry_ref[mine, HALF:] = own

    def group_join(m):
        @pl.when(lax.rem(m, 2) == 0)
        def _():
            core_copy(row, m // 2).wait_recv()
            for r in range(2):
                core_copy(r, m // 2).wait_send()

        pair_join(row, m)
        row_copy(m).wait_recv()
        early, late = ordered(is_row_late, pair_buf[row * PARTS + m], row_in[m])
        join(early, late, group_buf, m)

    def finish(m):
        own, far = descend(is_row_late, pair_buf[row * PARTS + m], row_in[m], enter_in[m],
                           leave_in[m])
        down_out[m, :HALF], down_out[m, HALF:] = far
        down_copy(m).start()
        final_level(row, m, *own)
        row_copy(m).wait_send()

    def down(m):
        down_copy(m).wait_recv()
        final_level(1 - row, m, down_in[m, :HALF], down_in[m, HALF:])

        @pl.when(m == PARTS - 1)
        def _():
            final_chunk(chunk_of(1 - row, m // 2, core))

    def take_back(r, m, wide):
        back_copy(r, m).wait_recv()
        carry_ref[part_of(r, m, 1 - core)] = back_in[r * PARTS + m]

        @pl.when(wide)
        def _():
            final_wide(m - 1 + r)

        back_copy(r, m).wait_send()

    def take_near(m):
        take_back(row, m, lax.rem(m, 2) == 1)

        @pl.when(jnp.logical_not(is_last))
        def _():
            enter_copy(m).wait_send()

        @pl.when(jnp.logical_not(is_first))
        def _():
            leave_copy(m).wait_send()

    def take_far(m):
        take_back(1 - row, m, (lax.rem(m, 2) == 1) & (m < PARTS - 1))

        @pl.when(m == PARTS - 1)
        def _():
            final_chunk(chunk_of(1 - row, m // 2, 1 - core))

        down_copy(m).wait_send()

    def stage(j, start, act):
        m = (j - start) // SPACING
        due = (j >= start) & (j < start + SPACING * PARTS) & (lax.rem(j - start, SPACING) == 0)

        @pl.when(due)
        def _():
            act(m)

    enter_start = JOIN_START + HOP * rank
    leave_start = JOIN_START + HOP * (ranks - 1 - rank)
    finish_start = jnp.maximum(enter_start, leave_start)
    down_start = finish_start + DOWN_LAG
    slots = JOIN_START + HOP * (ranks - 1) + DOWN_LAG + NEAR_LAG + SPACING * PARTS

    @pl.loop(0, slots)
    def _(j):
        stage(j, JOIN_START, group_join)
        stage(j, enter_start, take_enter)
        stage(j, leave_start, take_leave)
        stage(j, finish_start, finish)
        stage(j, finish_start + NEAR_LAG, take_near)
        stage(j, down_start, down)
        stage(j, down_start + NEAR_LAG, take_far)

        @pl.when(j < WIDES - EARLY)
        def _():
            local_step(j + EARLY)

        @pl.when(j == 0)
        def _():
            prepare_block()

        @pl.when(j < WIDES)
        def _():
            block_wide(2 * lax.rem(j, CHUNKS) + j // CHUNKS)

        @pl.when(j == WIDES)
        def _():
            first = lax.broadcasted_iota(jnp.int32, (BLOCK, BLOCK), 0)
            second = lax.broadcasted_iota(jnp.int32, (BLOCK, BLOCK), 1)
            pairs = jnp.where(first <= second, pairs_ref[...], 0.0).astype(BF16)
            read_sum[...] += contract(pairs, b_ref[...], 0, 0)
            write_sum[...] += contract(pairs, c_ref[...], 1, 0)

    read_ref[...] = read_sum[...].astype(BF16)
    write_ref[...] = write_sum[...].astype(BF16)
    heads = lax.broadcasted_iota(jnp.int32, (HEADS, 32), 0)
    chunks = lax.broadcasted_iota(jnp.int32, (HEADS, 32), 1)
    pick = jnp.where(heads // 2 == chunks, 1.0, 0.0).astype(BF16)
    ends = sum(contract(pick, part, 1, 0) for part in split_three(ends_ref[...]))
    heads = lax.broadcasted_iota(jnp.int32, (HEADS, 128), 0)
    entries = lax.broadcasted_iota(jnp.int32, (HEADS, 128), 1)
    own_head = entries // P_SIZE == lax.rem(heads, 2)
    total = jnp.sum(jnp.where(own_head, ends, 0.0), axis=1, keepdims=True)
    flows = flowrow_ref[...] + outdot_ref[...]
    decay_ref[...] = total + three_sums(flows, lower_ref[...], 0)


def whole_call(x, g, b, c, rates, ranks):
    half, one = 2 * PARTS, PARTS

    def buffer(count, rows):
        return pltpu.VMEM((count, rows, CHUNK), F32)

    def wide(dtype):
        return pltpu.VMEM((BLOCK, WIDTH), dtype)

    def square(dtype):
        return pltpu.VMEM((BLOCK, BLOCK), dtype)

    def parts():
        return pltpu.VMEM((BLOCK, 128), BF16)

    def rows():
        return pltpu.VMEM((HEADS, BLOCK), F32)

    counts = [one, one] + [one] * 8 + [half, half]
    return pl.pallas_call(
        functools.partial(whole_kernel, ranks),
        out_shape=[
            pltpu.VMEM((BLOCK, WIDTH), BF16),
            pltpu.VMEM((BLOCK, N), BF16),
            pltpu.VMEM((BLOCK, N), BF16),
            pltpu.VMEM((HEADS, BLOCK), F32),
        ],
        in_specs=[pl.BlockSpec(memory_space=pltpu.HBM)] * 5,
        out_specs=[pl.BlockSpec(memory_space=pltpu.VMEM)] * 4,
        scratch_shapes=[
            wide(BF16), wide(BF16), parts(), parts(), rows(),
            wide(BF16), wide(BF16), wide(F32), wide(F32), wide(F32),
            rows(), rows(), rows(), pltpu.VMEM((32, CHUNK), F32),
            pltpu.VMEM((BLOCK, N), F32), pltpu.VMEM((BLOCK, N), F32),
            parts(), parts(), parts(), parts(), pltpu.VMEM((BLOCK, 128), F32),
            pltpu.VMEM((128, WIDE), jnp.int32),
            pltpu.VMEM((N, BLOCK), BF16), pltpu.VMEM((N, BLOCK), BF16),
            buffer(2 * half, PAY), buffer(2 * half, 2 * HALF),
            square(BF16), square(BF16), square(BF16), pltpu.VMEM((4, SUB, SUB), F32), square(F32),
            buffer(half, PAY), buffer(half, PAY), buffer(one, PAY), buffer(one, PAY),
            buffer(one, HALF), buffer(one, HALF), buffer(one, HALF), buffer(one, HALF),
            buffer(one, 2 * HALF), buffer(one, 2 * HALF), buffer(half, 2 * HALF),
            buffer(half, 2 * HALF),
            pltpu.SemaphoreType.DMA((WIDES,)), pltpu.SemaphoreType.DMA((WIDES,)),
            pltpu.SemaphoreType.DMA((3,)),
        ] + [pltpu.SemaphoreType.DMA((count,)) for count in counts],
        compiler_params=pltpu.CompilerParams(
            vmem_limit_bytes=VMEM_BYTES, collective_id=0, has_side_effects=True
        ),
    )(x, g, b, c, rates)


def store_kernel(*refs):
    sources, targets, sems = refs[:4], refs[4:8], refs[8]
    copies = [
        pltpu.make_async_copy(source, target, sems.at[index])
        for index, (source, target) in enumerate(zip(sources, targets))
    ]
    for copy in copies:
        copy.start()
    for copy in copies:
        copy.wait()


def store_call(results):
    return pl.pallas_call(
        store_kernel,
        out_shape=[jax.ShapeDtypeStruct(result.shape, result.dtype) for result in results],
        in_specs=[pl.BlockSpec(memory_space=pl.ANY)] * 4,
        out_specs=[pl.BlockSpec(memory_space=pl.ANY)] * 4,
        scratch_shapes=[pltpu.SemaphoreType.DMA((4,))],
        compiler_params=pltpu.CompilerParams(vmem_limit_bytes=COPY_BYTES),
    )(*results)


def body(inputs, write_vectors, read_vectors, log_decay, grad_out, *, seq_size):
    results = whole_call(
        inputs, grad_out, write_vectors, read_vectors, log_decay, seq_size // 4
    )
    return tuple(store_call(results))


def solution(mesh):
    rows = P(("grp", "seq"), None)
    columns = P(None, ("grp", "seq"))
    return jax.shard_map(
        functools.partial(body, seq_size=mesh.shape["seq"]),
        mesh=mesh,
        in_specs=(rows, rows, rows, columns, rows),
        out_specs=(rows, rows, rows, columns),
        check_vma=False,
    )
```
